128 devices in a mesh: comp: 2 (over core), dom: 64 (over x, y, z).
Axes of the slice: x: 4, y: 4, z: 4, core: 2. Of those that a mesh axis runs over, the one named last changes fastest.
Arguments:
- ocean_state: float32 [4, 80, 65536], P(None, None, ('comp', 'dom')), may hold values from -6 to 6
- atm_flux: float32 [2, 4, 262144], P(None, None, ('comp', 'dom')), may hold values from -6 to 6
- edge_coeff: float32 [7, 65536], P(None, ('comp', 'dom')), may hold values from 0.015 to 0.085
- neighbours: int32 [7, 65536], P(None, ('comp', 'dom')), may hold values from 0 to 1023
- halo_send: int32 [2, 32768], P(None, ('comp', 'dom')), may hold values from 0 to 511
- send_idx: int32 [128, 1024], P(('comp', 'dom')), may hold values from 0 to 2047
- recv_slot: int32 [4, 65536], P(None, ('comp', 'dom')), may hold values from 0 to 1023
- regrid_weight: float32 [4, 65536], P(None, ('comp', 'dom')), may hold values from 0.1 to 1
Outputs:
- final_state: float32 [4, 80, 65536], P(None, None, ('comp', 'dom'))
- atm_surface: float32 [4, 262144], P(None, ('comp', 'dom'))
The draws below stay inside these ranges and needn't reach their ends.
Inputs may be any that keep to these rules, and one draw needn't show every extreme that they name: `halo_send`: local cell numbers of the sending partition. `neighbours`: values below 512 are the partition's own cells, the rest halo cells. `recv_slot`: slots of the partition's received buffer, which come only from partitions q-4 to q+3.
All inputs are finite; a program needn't handle non-finite values.
Results may differ from the reference program's by a relative error of at most 0.0001.
Values sent between devices are 32-bit elements; how exact they have to be, the bound alone decides.
A program may use at most 192 MiB of HBM per device.

```python
import math
import jax
import jax.numpy as jnp
from jax import lax

FIELDS = 4
LEVELS = 80
NEIGHBOURS = 7
SOURCES = 4
PEERS = 8
STEPS = 3
OCN_DEV = 512
ATM_DEV = 2048
HALO_DEV = 256
OCN = 65536
ATM = 262144
HALO = 32768
CAP = 128
SLOTS = 1024
N_COMP = 2
N_DOM = 64
DEVICES = 128


def with_ends(drawn, stream_key, smallest, high):
    longest = drawn.shape.index(max(drawn.shape))
    spots = []
    for shift in (0, 1):
        where = [jax.random.randint(jax.random.fold_in(stream_key, axis), (), 0, length) for axis, length in enumerate(drawn.shape)]
        where[longest] = (where[longest] + shift) % drawn.shape[longest]
        spots.append(tuple(where))
    return drawn.at[spots[0]].set(smallest).at[spots[1]].set(high)


def block_levels(key, shape, cuts, smallest, high):
    def one(dim, parts):
        heights = jax.random.uniform(jax.random.fold_in(jax.random.fold_in(key, 6), dim), (parts,), jnp.float32, smallest / len(cuts), high / len(cuts))
        return jnp.repeat(jnp.exp(heights), shape[dim] // parts).reshape((-1,) + (1,) * (len(shape) - dim - 1))

    gain = one(*cuts[0])
    for cut in cuts[1:]:
        gain = gain * one(*cut)
    return gain


def normal_values(stream_key, shape, deviation, most, cuts=(), held_as=jnp.bfloat16):
    entries = jax.random.normal(stream_key, shape, jnp.float32) * deviation
    if len(cuts) > 0:
        entries = block_levels(stream_key, shape, cuts, -0.22, 0.18) * entries
    return jnp.clip(entries, min=-most, max=most).astype(held_as)


def setup_inputs(seed: int = 0) -> dict:
    arg_keys = jax.random.split(jax.random.key(seed), 9)
    return {
        "ocean_state": normal_values(arg_keys[0], (FIELDS, LEVELS, OCN), 1.0, 6.0, ((2, 128),), jnp.float32),
        "atm_flux": normal_values(arg_keys[1], (2, FIELDS, ATM), 1.0, 6.0, ((2, 128),), jnp.float32),
        "edge_coeff": jnp.clip(jnp.exp(math.log(0.085) - 1.7346011 * jax.random.uniform(arg_keys[2], (NEIGHBOURS, OCN), jnp.float32) ** block_levels(arg_keys[2], (NEIGHBOURS, OCN), ((1, 128),), -0.2, 0.2)), 0.015, 0.085),
        "neighbours": with_ends(jax.random.randint(arg_keys[3], (NEIGHBOURS, OCN), 0, OCN_DEV + 2 * HALO_DEV), jax.random.fold_in(arg_keys[3], 1), 0, (OCN_DEV + 2 * HALO_DEV) - 1).astype(jnp.int32),
        "halo_send": with_ends(jax.random.randint(arg_keys[4], (2, HALO), 0, OCN_DEV), jax.random.fold_in(arg_keys[4], 1), 0, OCN_DEV - 1).astype(jnp.int32),
        "send_idx": with_ends(jax.random.randint(arg_keys[5], (DEVICES, SLOTS), 0, ATM_DEV), jax.random.fold_in(arg_keys[5], 1), 0, ATM_DEV - 1).astype(jnp.int32),
        "recv_slot": with_ends(jax.random.randint(arg_keys[6], (SOURCES, OCN), 0, SLOTS), jax.random.fold_in(arg_keys[6], 1), 0, SLOTS - 1).astype(jnp.int32),
        "regrid_weight": jnp.clip(jnp.exp(math.log(1.0) - 2.3025851 * jax.random.uniform(arg_keys[7], (SOURCES, OCN), jnp.float32) ** block_levels(arg_keys[7], (SOURCES, OCN), ((1, 128),), -0.2, 0.2)), 0.1, 1.0),
    }


vertical_mix = 0.2
forcing_scale = 0.1
relaxation = 0.25
penetration = 8.0
reach_below = 3


def advance(fields, extended, coeff, neighbour_tile, forcing_cells):
    accumulated = jnp.zeros_like(fields)
    for neighbour in range(neighbour_tile.shape[0]):
        beside = jnp.take(extended, neighbour_tile[neighbour], axis=2)
        accumulated = accumulated + coeff[neighbour][None, None, :] * (beside - fields)
    shallower = jnp.concatenate([fields[:, :1], fields[:, :-1]], axis=1)
    deeper = jnp.concatenate([fields[:, 1:], fields[:, -1:]], axis=1)
    depth = jnp.arange(fields.shape[1]).astype(fields.dtype)
    profile = jnp.exp(-depth / penetration)
    return (fields + accumulated + vertical_mix * (shallower - fields) + vertical_mix * (deeper - fields)
            + forcing_scale * forcing_cells[:, None, :] * profile[None, :, None])


def interpolate(received, slot_table, weights):
    accumulated = jnp.zeros((received.shape[0], slot_table.shape[1]), received.dtype)
    for source in range(slot_table.shape[0]):
        accumulated = accumulated + weights[source][None, :] * jnp.take(received, slot_table[source], axis=1)
    return accumulated


def spread(surface, slot_table, weights, slot_count):
    values = jnp.concatenate([weights[source][:, None] * surface.T for source in range(slot_table.shape[0])], axis=0)
    return jax.ops.segment_sum(values, slot_table.reshape(-1), num_segments=slot_count).T


def reference(ocean_state, atm_flux, edge_coeff, neighbours, halo_send, send_idx, recv_slot, regrid_weight):
    device_count = N_COMP * N_DOM

    def per_device(array):
        split = array.reshape(array.shape[:-1] + (device_count, -1))
        return jnp.moveaxis(split, -2, 0)

    def joined(array):
        moved = jnp.moveaxis(array, 0, -2)
        return moved.reshape(moved.shape[:-2] + (-1,))

    def to_peers(outgoing, sign):
        shaped = outgoing.reshape(device_count, outgoing.shape[1], PEERS, CAP)
        pieces = [jnp.roll(shaped[:, :, peer], sign * (peer - reach_below), axis=0) for peer in range(PEERS)]
        return jnp.stack(pieces, axis=2).reshape(device_count, outgoing.shape[1], -1)

    def take_points(values, order):
        return jnp.take(values, order, axis=1)

    def take_rims(values, order):
        return jnp.take(values, order, axis=2)

    def collect(back, order):
        return jax.ops.segment_sum(back.T, order, num_segments=ATM_DEV).T

    def spread_one(surface, slot_table, weights):
        return spread(surface, slot_table, weights, SLOTS)

    def advance_packed(packed):
        return advance(*packed)

    fields = per_device(ocean_state)
    coeff = per_device(edge_coeff)
    tiles = per_device(neighbours)
    outward = per_device(halo_send).reshape(device_count, -1)
    slot_tables = per_device(recv_slot)
    weights = per_device(regrid_weight)
    atmosphere = per_device(atm_flux)
    returned = jnp.zeros((device_count, FIELDS, ATM_DEV), jnp.float32)
    for interval in range(2):
        forcing = atmosphere[:, interval] - relaxation * returned
        received = to_peers(jax.vmap(take_points)(forcing, send_idx), 1)
        forcing_cells = jax.vmap(interpolate)(received, slot_tables, weights)
        for substep in range(STEPS):
            rim_values = jax.vmap(take_rims)(fields, outward)
            from_lower = jnp.roll(rim_values, 1, axis=0)[..., HALO_DEV:]
            from_upper = jnp.roll(rim_values, -1, axis=0)[..., :HALO_DEV]
            extended = jnp.concatenate([fields, from_lower, from_upper], axis=3)
            fields = lax.map(advance_packed, (fields, extended, coeff, tiles, forcing_cells))
        slot_sums = jax.vmap(spread_one)(fields[:, :, 0, :], slot_tables, weights)
        returned = jax.vmap(collect)(to_peers(slot_sums, -1), send_idx)
    return joined(fields), joined(returned)
```

```python
import jax
import jax.numpy as jnp
from jax import lax
from jax.sharding import PartitionSpec as P

PEERS = 8
STEPS = 3

vertical_mix = 0.2
forcing_scale = 0.1
relaxation = 0.25
penetration = 8.0
reach_below = 3
AXES = ("comp", "dom")


def passed_along(shard, by):
    peers = lax.axis_size(AXES)
    return lax.ppermute(shard, AXES, [(i, (i + by) % peers) for i in range(peers)])


def product(left, right):
    return jnp.dot(left, right, precision=lax.Precision.HIGH, preferred_element_type=jnp.float32)


def product_t(left, right):
    return lax.dot_general(
        left,
        right,
        (((1,), (1,)), ((), ())),
        precision=lax.Precision.HIGH,
        preferred_element_type=jnp.float32,
    )


def selector(index, rows, weights=None):
    total = None
    place = jnp.arange(rows, dtype=jnp.int32)[:, None]
    for n in range(index.shape[0]):
        value = 1.0 if weights is None else weights[n][None, :]
        term = jnp.where(index[n][None, :] == place, value, 0.0)
        total = term if total is None else total + term
    return total


def moved_slots(values, sign):
    pieces = values.reshape(values.shape[0], PEERS, -1)
    moved = [passed_along(pieces[:, j], sign * (j - reach_below)) for j in range(PEERS)]
    return jnp.stack(moved, axis=1).reshape(values.shape[0], -1)


def shards(
    ocean_state, atm_flux, edge_coeff, neighbours, halo_send, send_idx, recv_slot, regrid_weight
):
    fields, levels, cells = ocean_state.shape
    points = atm_flux.shape[2]
    rim = halo_send.shape[1]
    slots = send_idx.shape[1]
    mix = selector(neighbours, cells + 2 * rim, edge_coeff)
    keep = 1.0 - 2.0 * vertical_mix - jnp.sum(edge_coeff, axis=0)
    rims = selector(halo_send.reshape(1, -1), cells)
    points_to_slots = selector(send_idx, points)
    slots_to_cells = selector(recv_slot, slots, regrid_weight)
    profile = forcing_scale * jnp.exp(-jnp.arange(levels).astype(jnp.float32) / penetration)
    state = ocean_state
    returned = jnp.zeros((fields, points), jnp.float32)
    for interval in range(2):
        forcing = atm_flux[interval] - relaxation * returned
        received = moved_slots(product(forcing, points_to_slots), 1)
        added = product(received, slots_to_cells)
        for step in range(STEPS):
            flat = state.reshape(fields * levels, cells)
            edge = product(flat, rims)
            upper = passed_along(edge[:, :rim], -1)
            lower = passed_along(edge[:, rim:], 1)
            extended = jnp.concatenate([flat, lower, upper], axis=1)
            beside = product(extended, mix).reshape(state.shape)
            shallower = jnp.concatenate([state[:, :1], state[:, :-1]], axis=1)
            deeper = jnp.concatenate([state[:, 1:], state[:, -1:]], axis=1)
            state = (
                keep[None, None, :] * state
                + beside
                + vertical_mix * (shallower + deeper)
                + added[:, None, :] * profile[None, :, None]
            )
        slot_sums = product_t(state[:, 0, :], slots_to_cells)
        returned = product_t(moved_slots(slot_sums, -1), points_to_slots)
    return (state, returned)


def solution(mesh):
    placed = (
        P(None, None, AXES),
        P(None, None, AXES),
        P(None, AXES),
        P(None, AXES),
        P(None, AXES),
        P(AXES, None),
        P(None, AXES),
        P(None, AXES),
    )
    return jax.shard_map(
        shards,
        mesh=mesh,
        in_specs=placed,
        out_specs=(P(None, None, AXES), P(None, AXES)),
        check_vma=False,
    )
```

```python
import jax
import jax.numpy as jnp
from jax import lax
from jax.experimental import pallas as pl
from jax.experimental.pallas import tpu as pltpu
from jax.sharding import PartitionSpec as P

AXES = ("comp", "dom")
MESH = pl.DeviceIdType.MESH
F32 = jnp.float32
BF16 = jnp.bfloat16

PEERS = 8
REACH = 3
STEPS = 3
GROUP = 4
LANES = 128

vertical_mix = 0.2
forcing_scale = 0.1
relaxation = 0.25
penetration = 8.0


def split(value):
    high = value.astype(BF16)
    return high, (value - high.astype(F32)).astype(BF16)


def across(left, right):
    return lax.dot_general(left, right, (((1,), (1,)), ((), ())), preferred_element_type=F32)


def lookup(table, index):
    return jnp.take_along_axis(table, index, axis=1, mode="promise_in_bounds")


def kernel(
    ocean, flux, coeff_in, near_in, halo_in, send_in, slot_in, weight_in,
    out_state, out_atm,
    state, parts, wide_hi, wide_lo, rims, coeff, near, halo, slots, weights,
    sends, air, sends8, keep, profile, added,
    slot_lanes, point_lanes, outgoing, arrived, surface, owned, sums, back, returned,
    rim_out, rim_in,
    state_send, state_recv, table_send, table_recv, flux_send, flux_recv,
    surf_send, surf_recv, back_send, back_recv, rim_send, rim_recv, out_send, out_recv, local,
):
    levels, cells = state.shape[1:]
    rim = halo.shape[2]
    points = air.shape[2]
    fields = GROUP
    blocks = points // LANES
    doms = lax.axis_size("dom")
    total = lax.axis_size("comp") * doms
    me = lax.axis_index("comp") * doms + lax.axis_index("dom")
    z = lax.rem(me, GROUP)
    base = me - z

    def device(p):
        p = lax.rem(p + total, total)
        return (lax.div(p, doms), lax.rem(p, doms))

    def remote(src, dst, send, recv, p):
        return pltpu.make_async_remote_copy(
            src_ref=src, dst_ref=dst, send_sem=send, recv_sem=recv,
            device_id=device(p), device_id_type=MESH,
        )

    barrier = pltpu.get_barrier_semaphore()
    for r in range(3):
        for k in range(GROUP):
            if r == 1 and k == 0:
                continue
            far = base + GROUP * (r - 1) + lax.rem(z + k, GROUP)
            pl.semaphore_signal(barrier, inc=1, device_id=device(far), device_id_type=MESH)

    tables = [(coeff_in, coeff), (near_in, near), (halo_in, halo), (slot_in, slots), (weight_in, weights)]
    own = [
        pltpu.make_async_copy(send_in, sends, local.at[0]),
        pltpu.make_async_copy(flux, air, local.at[1]),
        pltpu.make_async_copy(ocean.at[z], state.at[z], local.at[2]),
    ] + [
        pltpu.make_async_copy(src, dst.at[z], local.at[3 + n])
        for n, (src, dst) in enumerate(tables)
    ]
    for copy in own:
        copy.start()

    pl.semaphore_wait(barrier, 3 * GROUP - 1)

    for d in range(1, GROUP):
        far = lax.rem(z + d, GROUP)
        for n, (src, dst) in enumerate(tables):
            remote(src, dst.at[z], table_send.at[n, far], table_recv.at[n, z], base + far).start()
        remote(ocean.at[far], state.at[z], state_send.at[far], state_recv.at[z], base + far).start()

    def gather_and_send(interval):
        low = sends8[...] & (LANES - 1)
        high = lax.shift_right_logical(sends8[...], 7)
        for f in range(fields):
            total_f = jnp.zeros((PEERS, LANES), F32)
            for b in range(blocks):
                row = air[interval, f : f + 1, b * LANES : (b + 1) * LANES]
                if interval:
                    at = f * blocks + b
                    row = row - relaxation * returned[at : at + 1, :]
                table = jnp.broadcast_to(row, (PEERS, LANES))
                total_f = jnp.where(high == b, lookup(table, low), total_f)
            moved = pltpu.roll(
                jnp.concatenate([total_f, jnp.zeros((PEERS, LANES), F32)], axis=0), z + 1, 0
            )
            for r in range(3):
                outgoing[interval, f, r] = moved[GROUP * r : GROUP * (r + 1), :]
        for r in range(3):
            for k in range(GROUP):
                f = lax.rem(z + k, GROUP)
                src = outgoing.at[interval, f, r]
                dst = arrived.at[interval, GROUP * (2 - r) + z]
                if r == 1 and k == 0:
                    pltpu.make_async_copy(src, dst, local.at[8 + interval]).start()
                else:
                    remote(
                        src, dst, flux_send.at[interval, GROUP * r + f],
                        flux_recv.at[interval, GROUP * (2 - r) + z],
                        base + GROUP * (r - 1) + f,
                    ).start()

    def receive_forcing(interval):
        for r in range(3):
            for k in range(GROUP):
                f = lax.rem(z + k, GROUP)
                src = outgoing.at[interval, f, r]
                dst = arrived.at[interval, GROUP * r + f]
                if r == 1 and k == 0:
                    pltpu.make_async_copy(src, dst, local.at[8 + interval]).wait()
                else:
                    copy = remote(
                        src, dst, flux_send.at[interval, GROUP * r + f],
                        flux_recv.at[interval, GROUP * r + f], base + GROUP * (r - 1) + f,
                    )
                    copy.wait_recv()
                    copy.wait_send()
        for i in range(GROUP):
            for pair in range(cells // (2 * LANES)):
                cols = [slice((2 * pair + h) * LANES, (2 * pair + h + 1) * LANES) for h in range(2)]
                index = jnp.concatenate([slots[i, :, c] for c in cols], axis=0)
                weight = jnp.concatenate([weights[i, :, c] for c in cols], axis=0)
                low = index & (LANES - 1)
                high = lax.shift_right_logical(index, 7)
                value = jnp.zeros((PEERS, LANES), F32)
                for j in range(PEERS):
                    row = arrived[interval, 7 + i - j, i : i + 1, :]
                    table = jnp.broadcast_to(row, (PEERS, LANES))
                    value = jnp.where(high == j, lookup(table, low), value)
                value = value * weight
                for h in range(2):
                    added[i, :, cols[h]] = jnp.sum(value[4 * h : 4 * h + 4], axis=0, keepdims=True)

    def surface_out(interval):
        for i in range(GROUP):
            surface[interval, i] = state[i, 0:1, :]
        for d in range(GROUP):
            far = lax.rem(z + d, GROUP)
            if d == 0:
                pltpu.make_async_copy(
                    surface.at[interval, z], owned.at[interval, z], local.at[10 + interval]
                ).start()
            else:
                remote(
                    surface.at[interval, far], owned.at[interval, z],
                    surf_send.at[interval, far], surf_recv.at[interval, z], base + far,
                ).start()

    def sums_out(interval):
        for d in range(GROUP):
            far = lax.rem(z + d, GROUP)
            if d == 0:
                pltpu.make_async_copy(
                    surface.at[interval, z], owned.at[interval, z], local.at[10 + interval]
                ).wait()
            else:
                copy = remote(
                    surface.at[interval, far], owned.at[interval, far],
                    surf_send.at[interval, far], surf_recv.at[interval, far], base + far,
                )
                copy.wait_recv()
                copy.wait_send()
        acc = jnp.zeros((2 * fields * PEERS, LANES), F32)
        place = lax.broadcasted_iota(jnp.int32, (PEERS, cells), 0)
        for k in range(slots.shape[1]):
            hit = lax.shift_right_logical(slots[z, k : k + 1, :], 7) == place
            rows = [
                jnp.where(hit, weights[z, k : k + 1, :] * owned[interval, f], 0.0)
                for f in range(fields)
            ]
            high, low = split(jnp.concatenate(rows, axis=0))
            acc = acc + across(jnp.concatenate([high, low], axis=0), slot_lanes[k])
        acc = acc[: fields * PEERS] + acc[fields * PEERS :]
        for f in range(fields):
            for j in range(PEERS):
                sums[interval, j, f] = acc[f * PEERS + j : f * PEERS + j + 1, :]
        for j in range(PEERS):
            if j == REACH:
                pltpu.make_async_copy(
                    sums.at[interval, j], back.at[interval, j], local.at[12 + interval]
                ).start()
            else:
                remote(
                    sums.at[interval, j], back.at[interval, j],
                    back_send.at[interval, j], back_recv.at[interval, j], me + (REACH - j),
                ).start()

    def collect(interval):
        for j in range(PEERS):
            if j == REACH:
                pltpu.make_async_copy(
                    sums.at[interval, j], back.at[interval, j], local.at[12 + interval]
                ).wait()
            else:
                copy = remote(
                    sums.at[interval, j], back.at[interval, j],
                    back_send.at[interval, j], back_recv.at[interval, j], me + (REACH - j),
                )
                copy.wait_recv()
                copy.wait_send()
        place = lax.broadcasted_iota(jnp.int32, (blocks, LANES), 0)
        columns = []
        for j in range(PEERS):
            hit = lax.shift_right_logical(sends[:, j * LANES : (j + 1) * LANES], 7) == place
            columns.append(
                jnp.concatenate(
                    [jnp.where(hit, back[interval, j, f], 0.0) for f in range(fields)], axis=0
                )
            )
        high, low = split(jnp.concatenate(columns, axis=1))
        both = across(jnp.concatenate([high, low], axis=0), point_lanes[...])
        returned[...] = both[: fields * blocks] + both[fields * blocks :]

    def set_parts(i, value):
        high, low = split(value)
        parts[i, 0:levels, 0:cells] = high
        parts[i, levels : 2 * levels, 0:cells] = low

    def rims_of(t, i):
        edge = jnp.dot(parts[i, :, 0:cells], rims[i], preferred_element_type=F32)
        if i > 0:
            parts[i - 1, :, cells + rim : cells + 2 * rim] = edge[:, 0:rim].astype(BF16)
        else:
            rim_out[t, 0] = edge[0:levels, 0:rim] + edge[levels:, 0:rim]
            remote(
                rim_out.at[t, 0], rim_in.at[t, 1], rim_send.at[t, 0], rim_recv.at[t, 1], me - GROUP
            ).start()
        if i < GROUP - 1:
            parts[i + 1, :, cells : cells + rim] = edge[:, rim : 2 * rim].astype(BF16)
        else:
            rim_out[t, 1] = edge[0:levels, rim : 2 * rim] + edge[levels:, rim : 2 * rim]
            remote(
                rim_out.at[t, 1], rim_in.at[t, 0], rim_send.at[t, 1], rim_recv.at[t, 0], me + GROUP
            ).start()

    def rim_arrives(t, side):
        p = me + (GROUP if side else -GROUP)
        copy = remote(
            rim_out.at[t, 1 - side], rim_in.at[t, side], rim_send.at[t, 1 - side],
            rim_recv.at[t, side], p,
        )
        copy.wait_recv()
        high, low = split(rim_in[t, side])
        i, start = (GROUP - 1, cells + rim) if side else (0, cells)
        parts[i, 0:levels, start : start + rim] = high
        parts[i, levels : 2 * levels, start : start + rim] = low

    def rims_sent(t):
        remote(
            rim_out.at[t, 0], rim_in.at[t, 1], rim_send.at[t, 0], rim_recv.at[t, 1], me - GROUP
        ).wait_send()
        remote(
            rim_out.at[t, 1], rim_in.at[t, 0], rim_send.at[t, 1], rim_recv.at[t, 0], me + GROUP
        ).wait_send()

    def mixed(i):
        both = jnp.dot(parts[i], wide_hi[i], preferred_element_type=F32)
        small = jnp.dot(parts[i, 0:levels, :], wide_lo[i], preferred_element_type=F32)
        here = state[i]
        row = lax.broadcasted_iota(jnp.int32, (levels, cells), 0)
        above = jnp.where(row == 0, here, pltpu.roll(here, 1, 0))
        below = jnp.where(row == levels - 1, here, pltpu.roll(here, levels - 1, 0))
        return (
            keep[i] * here
            + (both[0:levels] + both[levels:] + small)
            + vertical_mix * (above + below)
        )

    def push(i):
        return added[i] * profile[...]

    level = lax.broadcasted_iota(jnp.int32, (levels, cells), 0).astype(F32)
    profile[...] = forcing_scale * jnp.exp(-level / penetration)
    own[0].wait()
    own[1].wait()
    sends8[...] = jnp.concatenate(
        [sends[:, j * LANES : (j + 1) * LANES] for j in range(PEERS)], axis=0
    )
    gather_and_send(0)
    for copy in own[3:]:
        copy.wait()

    def build(i):
        rows = [coeff[i, n : n + 1, :] for n in range(near.shape[1])]
        ids = [near[i, n : n + 1, :] for n in range(near.shape[1])]
        summed = []
        for n in range(len(rows)):
            value = rows[n]
            for m in range(n):
                value = value + jnp.where(ids[m] == ids[n], rows[m], 0.0)
            summed.append(value)
        whole = rows[0]
        for n in range(1, len(rows)):
            whole = whole + rows[n]
        keep[i] = (1.0 - 2.0 * vertical_mix) - whole
        step = 32

        def fill(c, _):
            first = pl.multiple_of(c * step, step)
            for q in range(cells // LANES):
                cols = slice(q * LANES, (q + 1) * LANES)
                place = lax.broadcasted_iota(jnp.int32, (step, LANES), 0) + first
                value = jnp.zeros((step, LANES), F32)
                for n in range(len(rows)):
                    value = jnp.where(ids[n][:, cols] == place, summed[n][:, cols], value)
                high, low = split(value)
                wide_hi[i, pl.ds(first, step), cols] = high
                wide_lo[i, pl.ds(first, step), cols] = low
            return 0

        lax.fori_loop(0, (cells + 2 * rim) // step, fill, 0)

        def select(c, _):
            first = pl.multiple_of(c * step, step)
            place = lax.broadcasted_iota(jnp.int32, (step, rim), 0) + first
            for side in range(2):
                hit = halo[i, side : side + 1, :] == place
                rims[i, pl.ds(first, step), side * rim : (side + 1) * rim] = jnp.where(
                    hit, 1.0, 0.0
                ).astype(BF16)
            return 0

        lax.fori_loop(0, cells // step, select, 0)

    def build_all(d, _):
        i = lax.rem(z + d, GROUP)

        @pl.when(d > 0)
        def _():
            for n, (src, dst) in enumerate(tables):
                copy = remote(src, dst.at[i], table_send.at[n, i], table_recv.at[n, i], base + i)
                copy.wait_recv()
                copy.wait_send()

        build(i)
        return 0

    lax.fori_loop(0, GROUP, build_all, 0)

    place = lax.broadcasted_iota(jnp.int32, (LANES, cells), 0)
    for k in range(slots.shape[1]):
        hit = (slots[z, k : k + 1, :] & (LANES - 1)) == place
        slot_lanes[k] = jnp.where(hit, 1.0, 0.0).astype(BF16)
    for h in range(sends.shape[1] // cells):
        hit = (sends[:, h * cells : (h + 1) * cells] & (LANES - 1)) == place
        point_lanes[:, h * cells : (h + 1) * cells] = jnp.where(hit, 1.0, 0.0).astype(BF16)

    own[2].wait()
    for d in range(1, GROUP):
        far = lax.rem(z + d, GROUP)
        copy = remote(
            ocean.at[far], state.at[far], state_send.at[far], state_recv.at[far], base + far
        )
        copy.wait_recv()
        copy.wait_send()
    for i in range(GROUP):
        set_parts(i, state[i])

    for interval in range(2):
        t = STEPS * interval
        if interval:
            surface_out(0)
        for i in (0, 3, 1, 2):
            rims_of(t, i)
        if interval:
            sums_out(0)
        for i in (1, 2):
            state[i] = mixed(i)
        if interval:
            collect(0)
            gather_and_send(1)
        rim_arrives(t, 0)
        state[0] = mixed(0)
        rim_arrives(t, 1)
        state[3] = mixed(3)
        rims_sent(t)
        receive_forcing(interval)
        for i in range(GROUP):
            value = state[i] + push(i)
            state[i] = value
            set_parts(i, value)

        def plain(s, _):
            now = t + s
            for i in (0, 3, 1, 2):
                rims_of(now, i)
            for i in (1, 2):
                value = mixed(i) + push(i)
                state[i] = value
                set_parts(i, value)
            rim_arrives(now, 0)
            value = mixed(0) + push(0)
            state[0] = value
            set_parts(0, value)
            rim_arrives(now, 1)
            value = mixed(3) + push(3)
            state[3] = value
            set_parts(3, value)
            rims_sent(now)
            return 0

        lax.fori_loop(1, STEPS, plain, 0)

    surface_out(1)
    for d in range(1, GROUP):
        far = lax.rem(z + d, GROUP)
        remote(
            state.at[far], out_state.at[z], out_send.at[far], out_recv.at[z], base + far
        ).start()
    mine = pltpu.make_async_copy(state.at[z], out_state.at[z], local.at[14])
    mine.start()
    sums_out(1)
    collect(1)
    out_atm[...] = returned[...]
    mine.wait()
    for d in range(1, GROUP):
        far = lax.rem(z + d, GROUP)
        copy = remote(
            state.at[far], out_state.at[far], out_send.at[far], out_recv.at[far], base + far
        )
        copy.wait_recv()
        copy.wait_send()


def shards(
    ocean_state, atm_flux, edge_coeff, neighbours, halo_send, send_idx, recv_slot, regrid_weight
):
    fields, levels, cells = ocean_state.shape
    points = atm_flux.shape[2]
    rim = halo_send.shape[1]
    slot_count = send_idx.shape[1]
    near = neighbours.shape[0]
    sources = recv_slot.shape[0]
    wide = cells + 2 * rim
    steps = 2 * STEPS
    dma = pltpu.SemaphoreType.DMA
    final, atm = pl.pallas_call(
        kernel,
        out_shape=(
            jax.ShapeDtypeStruct((fields, levels, cells), F32),
            jax.ShapeDtypeStruct((fields * points // LANES, LANES), F32),
        ),
        in_specs=[pl.BlockSpec(memory_space=pl.ANY)] * 8,
        out_specs=(
            pl.BlockSpec(memory_space=pl.ANY),
            pl.BlockSpec(memory_space=pltpu.VMEM),
        ),
        scratch_shapes=[
            pltpu.VMEM((GROUP, levels, cells), F32),
            pltpu.VMEM((GROUP, 2 * levels, wide), BF16),
            pltpu.VMEM((GROUP, wide, cells), BF16),
            pltpu.VMEM((GROUP, wide, cells), BF16),
            pltpu.VMEM((GROUP, cells, 2 * rim), BF16),
            pltpu.VMEM((GROUP, near, cells), F32),
            pltpu.VMEM((GROUP, near, cells), jnp.int32),
            pltpu.VMEM((GROUP, 2, rim), jnp.int32),
            pltpu.VMEM((GROUP, sources, cells), jnp.int32),
            pltpu.VMEM((GROUP, sources, cells), F32),
            pltpu.VMEM((1, slot_count), jnp.int32),
            pltpu.VMEM((2, fields, points), F32),
            pltpu.VMEM((PEERS, LANES), jnp.int32),
            pltpu.VMEM((GROUP, 1, cells), F32),
            pltpu.VMEM((levels, cells), F32),
            pltpu.VMEM((GROUP, 1, cells), F32),
            pltpu.VMEM((sources, LANES, cells), BF16),
            pltpu.VMEM((LANES, slot_count), BF16),
            pltpu.VMEM((2, fields, 3, GROUP, LANES), F32),
            pltpu.VMEM((2, 3 * GROUP, GROUP, LANES), F32),
            pltpu.VMEM((2, GROUP, 1, cells), F32),
            pltpu.VMEM((2, GROUP, 1, cells), F32),
            pltpu.VMEM((2, PEERS, fields, 1, LANES), F32),
            pltpu.VMEM((2, PEERS, fields, 1, LANES), F32),
            pltpu.VMEM((fields * points // LANES, LANES), F32),
            pltpu.VMEM((steps, 2, levels, rim), F32),
            pltpu.VMEM((steps, 2, levels, rim), F32),
            dma((GROUP,)),
            dma((GROUP,)),
            dma((5, GROUP)),
            dma((5, GROUP)),
            dma((2, 3 * GROUP)),
            dma((2, 3 * GROUP)),
            dma((2, GROUP)),
            dma((2, GROUP)),
            dma((2, PEERS)),
            dma((2, PEERS)),
            dma((steps, 2)),
            dma((steps, 2)),
            dma((GROUP,)),
            dma((GROUP,)),
            dma((15,)),
        ],
        compiler_params=pltpu.CompilerParams(
            collective_id=0, has_side_effects=True, vmem_limit_bytes=48 * 1024 * 1024
        ),
        name="coupled",
    )(
        ocean_state, atm_flux, edge_coeff, neighbours, halo_send, send_idx, recv_slot,
        regrid_weight,
    )
    return final, atm.reshape(fields, points)


def solution(mesh):
    placed = (
        P(None, None, AXES),
        P(None, None, AXES),
        P(None, AXES),
        P(None, AXES),
        P(None, AXES),
        P(AXES, None),
        P(None, AXES),
        P(None, AXES),
    )
    return jax.shard_map(
        shards,
        mesh=mesh,
        in_specs=placed,
        out_specs=(P(None, None, AXES), P(None, AXES)),
        check_vma=False,
    )
```

```python
import jax
import jax.numpy as jnp
from jax import lax
from jax.experimental import pallas as pl
from jax.experimental.pallas import tpu as pltpu
from jax.sharding import PartitionSpec as P

AXES = ("comp", "dom")
MESH = pl.DeviceIdType.MESH
F32 = jnp.float32
BF16 = jnp.bfloat16

PEERS = 8
REACH = 3
STEPS = 3
GROUP = 4
LANES = 128

vertical_mix = 0.2
forcing_scale = 0.1
relaxation = 0.25
penetration = 8.0


def split(value):
    high = value.astype(BF16)
    return high, (value - high.astype(F32)).astype(BF16)


def across(left, right):
    return lax.dot_general(left, right, (((1,), (1,)), ((), ())), preferred_element_type=F32)


def lookup(table, index):
    return jnp.take_along_axis(table, index, axis=1, mode="promise_in_bounds")


def kernel(
    ocean, flux, coeff_in, near_in, halo_in, send_in, slot_in, weight_in,
    out_state, out_atm,
    state, parts, wide_hi, wide_lo, rims, coeff, near, halo, slots, weights,
    sends, air, sends8, keep, profile, added,
    slot_lanes, point_lanes, outgoing, arrived, sums, back, returned,
    rim_out, rim_in, early,
    state_send, state_recv, table_send, table_recv, flux_send, flux_recv,
    back_send, back_recv, rim_send, rim_recv, out_send, out_recv, local,
):
    levels, cells = state.shape[1:]
    rim = halo.shape[2]
    points = air.shape[2]
    fields = GROUP
    blocks = points // LANES
    doms = lax.axis_size("dom")
    total = lax.axis_size("comp") * doms
    me = lax.axis_index("comp") * doms + lax.axis_index("dom")
    z = lax.rem(me, GROUP)
    base = me - z

    def device(p):
        p = lax.rem(p + total, total)
        return (lax.div(p, doms), lax.rem(p, doms))

    def remote(src, dst, send, recv, p):
        return pltpu.make_async_remote_copy(
            src_ref=src, dst_ref=dst, send_sem=send, recv_sem=recv,
            device_id=device(p), device_id_type=MESH,
        )

    barrier = pltpu.get_barrier_semaphore()
    for r in range(3):
        for k in range(GROUP):
            if r == 1 and k == 0:
                continue
            far = base + GROUP * (r - 1) + lax.rem(z + k, GROUP)
            pl.semaphore_signal(barrier, inc=1, device_id=device(far), device_id_type=MESH)

    tables = [(coeff_in, coeff), (near_in, near), (halo_in, halo), (slot_in, slots), (weight_in, weights)]
    own = [
        pltpu.make_async_copy(send_in, sends, local.at[0]),
        pltpu.make_async_copy(flux, air, local.at[1]),
        pltpu.make_async_copy(ocean.at[z], state.at[z], local.at[2]),
    ] + [
        pltpu.make_async_copy(src, dst.at[z], local.at[3 + n])
        for n, (src, dst) in enumerate(tables)
    ]
    for copy in own:
        copy.start()

    def gather(interval):
        low = sends8[...] & (LANES - 1)
        high = lax.shift_right_logical(sends8[...], 7)
        for f in range(fields):
            total_f = jnp.zeros((PEERS, LANES), F32)
            for b in range(blocks):
                row = air[interval, f : f + 1, b * LANES : (b + 1) * LANES]
                if interval:
                    at = f * blocks + b
                    row = row - relaxation * returned[at : at + 1, :]
                table = jnp.broadcast_to(row, (PEERS, LANES))
                total_f = jnp.where(high == b, lookup(table, low), total_f)
            moved = pltpu.roll(
                jnp.concatenate([total_f, jnp.zeros((PEERS, LANES), F32)], axis=0), z + 1, 0
            )
            for r in range(3):
                outgoing[interval, f, r] = moved[GROUP * r : GROUP * (r + 1), :]

    def send_slots(interval):
        for r in range(3):
            for k in range(GROUP):
                f = lax.rem(z + k, GROUP)
                src = outgoing.at[interval, f, r]
                dst = arrived.at[interval, GROUP * (2 - r) + z]
                if r == 1 and k == 0:
                    pltpu.make_async_copy(src, dst, local.at[8 + interval]).start()
                else:
                    remote(
                        src, dst, flux_send.at[interval, GROUP * r + f],
                        flux_recv.at[interval, GROUP * (2 - r) + z],
                        base + GROUP * (r - 1) + f,
                    ).start()

    def receive_forcing(interval):
        for r in range(3):
            for k in range(GROUP):
                f = lax.rem(z + k, GROUP)
                src = outgoing.at[interval, f, r]
                dst = arrived.at[interval, GROUP * r + f]
                if r == 1 and k == 0:
                    pltpu.make_async_copy(src, dst, local.at[8 + interval]).wait()
                else:
                    copy = remote(
                        src, dst, flux_send.at[interval, GROUP * r + f],
                        flux_recv.at[interval, GROUP * r + f], base + GROUP * (r - 1) + f,
                    )
                    copy.wait_recv()
                    copy.wait_send()
        for i in range(GROUP):
            for pair in range(cells // (2 * LANES)):
                cols = [slice((2 * pair + h) * LANES, (2 * pair + h + 1) * LANES) for h in range(2)]
                index = jnp.concatenate([slots[i, :, c] for c in cols], axis=0)
                weight = jnp.concatenate([weights[i, :, c] for c in cols], axis=0)
                low = index & (LANES - 1)
                high = lax.shift_right_logical(index, 7)
                value = jnp.zeros((PEERS, LANES), F32)
                for j in range(PEERS):
                    row = arrived[interval, 7 + i - j, i : i + 1, :]
                    table = jnp.broadcast_to(row, (PEERS, LANES))
                    value = jnp.where(high == j, lookup(table, low), value)
                value = value * weight
                for h in range(2):
                    added[i, :, cols[h]] = jnp.sum(value[4 * h : 4 * h + 4], axis=0, keepdims=True)

    def slot_sums(interval, i):
        place = lax.broadcasted_iota(jnp.int32, (PEERS, cells), 0)
        acc = jnp.zeros((2 * PEERS, LANES), F32)
        top = state[i, 0:1, :]
        for k in range(slots.shape[1]):
            hit = lax.shift_right_logical(slots[i, k : k + 1, :], 7) == place
            high, low = split(jnp.where(hit, weights[i, k : k + 1, :] * top, 0.0))
            acc = acc + across(jnp.concatenate([high, low], axis=0), slot_lanes[i, k])
        acc = acc[:PEERS] + acc[PEERS:]
        for j in range(PEERS):
            sums[interval, i - j + REACH + GROUP, i] = acc[j : j + 1, :]

    def back_copy(interval, r, k, start):
        f = lax.rem(z + k, GROUP)
        src = sums.at[interval, GROUP * r + f]
        if r == 1 and k == 0:
            dst = back.at[interval, GROUP + z]
            copy = pltpu.make_async_copy(src, dst, local.at[10 + interval])
            copy.start() if start else copy.wait()
            return
        send = back_send.at[interval, GROUP * r + f]
        p = base + GROUP * (r - 1) + f
        slot = GROUP * (2 - r) + z if start else GROUP * r + f
        copy = remote(src, back.at[interval, slot], send, back_recv.at[interval, slot], p)
        if start:
            copy.start()
        else:
            copy.wait_recv()
            copy.wait_send()

    def sums_out(interval):
        for r in range(3):
            for k in range(GROUP):
                back_copy(interval, r, k, True)

    def collect(interval):
        for r in range(3):
            for k in range(GROUP):
                back_copy(interval, r, k, False)
        place = lax.broadcasted_iota(jnp.int32, (blocks, LANES), 0)
        values = []
        for f in range(fields):
            rows = [back[interval, GROUP * r + f, i] for r in range(3) for i in range(GROUP)]
            rows.append(jnp.zeros((GROUP, LANES), F32))
            values.append(pltpu.roll(jnp.concatenate(rows, axis=0), 2 * PEERS - 1 - z, 0))
        columns = []
        for j in range(PEERS):
            hit = lax.shift_right_logical(sends[:, j * LANES : (j + 1) * LANES], 7) == place
            columns.append(
                jnp.concatenate(
                    [jnp.where(hit, values[f][j : j + 1, :], 0.0) for f in range(fields)], axis=0
                )
            )
        high, low = split(jnp.concatenate(columns, axis=1))
        both = across(jnp.concatenate([high, low], axis=0), point_lanes[...])
        returned[...] = both[: fields * blocks] + both[fields * blocks :]

    def set_parts(i, value):
        high, low = split(value)
        parts[i, 0:levels, 0:cells] = high
        parts[i, levels : 2 * levels, 0:cells] = low

    def rims_of(t, i):
        edge = jnp.dot(parts[i, :, 0:cells], rims[i], preferred_element_type=F32)
        if i > 0:
            parts[i - 1, :, cells + rim : cells + 2 * rim] = edge[:, 0:rim].astype(BF16)
        else:
            rim_out[t, 0] = edge[0:levels, 0:rim] + edge[levels:, 0:rim]
            remote(
                rim_out.at[t, 0], rim_in.at[t, 1], rim_send.at[t, 0], rim_recv.at[t, 1], me - GROUP
            ).start()
        if i < GROUP - 1:
            parts[i + 1, :, cells : cells + rim] = edge[:, rim : 2 * rim].astype(BF16)
        else:
            rim_out[t, 1] = edge[0:levels, rim : 2 * rim] + edge[levels:, rim : 2 * rim]
            remote(
                rim_out.at[t, 1], rim_in.at[t, 0], rim_send.at[t, 1], rim_recv.at[t, 0], me + GROUP
            ).start()

    def rim_arrives(t, side):
        p = me + (GROUP if side else -GROUP)
        copy = remote(
            rim_out.at[t, 1 - side], rim_in.at[t, side], rim_send.at[t, 1 - side],
            rim_recv.at[t, side], p,
        )
        copy.wait_recv()
        high, low = split(rim_in[t, side])
        i, start = (GROUP - 1, cells + rim) if side else (0, cells)
        both = jnp.dot(
            jnp.concatenate([high, low], axis=0), wide_hi[i, start : start + rim, :],
            preferred_element_type=F32,
        )
        small = jnp.dot(high, wide_lo[i, start : start + rim, :], preferred_element_type=F32)
        return early[side] + (both[0:levels] + both[levels:] + small)

    def rims_sent(t):
        remote(
            rim_out.at[t, 0], rim_in.at[t, 1], rim_send.at[t, 0], rim_recv.at[t, 1], me - GROUP
        ).wait_send()
        remote(
            rim_out.at[t, 1], rim_in.at[t, 0], rim_send.at[t, 1], rim_recv.at[t, 0], me + GROUP
        ).wait_send()

    def product(i, first, last):
        both = jnp.dot(
            parts[i, :, first:last], wide_hi[i, first:last, :], preferred_element_type=F32
        )
        small = jnp.dot(
            parts[i, 0:levels, first:last], wide_lo[i, first:last, :], preferred_element_type=F32
        )
        return both[0:levels] + both[levels:] + small

    def mixed(i):
        here = state[i]
        row = lax.broadcasted_iota(jnp.int32, (levels, cells), 0)
        above = jnp.where(row == 0, here, pltpu.roll(here, 1, 0))
        below = jnp.where(row == levels - 1, here, pltpu.roll(here, levels - 1, 0))
        value = keep[i] * here + vertical_mix * (above + below)
        if i == 0:
            return value + product(i, 0, cells) + product(i, cells + rim, cells + 2 * rim)
        if i == GROUP - 1:
            return value + product(i, 0, cells + rim)
        return value + product(i, 0, cells + 2 * rim)

    def push(i):
        return added[i] * profile[...]

    sums[...] = jnp.zeros_like(sums)
    level = lax.broadcasted_iota(jnp.int32, (levels, cells), 0).astype(F32)
    profile[...] = forcing_scale * jnp.exp(-level / penetration)
    own[0].wait()
    own[1].wait()
    sends8[...] = jnp.concatenate(
        [sends[:, j * LANES : (j + 1) * LANES] for j in range(PEERS)], axis=0
    )
    gather(0)
    pl.semaphore_wait(barrier, 3 * GROUP - 1)
    for d in range(1, GROUP):
        far = lax.rem(z + d, GROUP)
        for n, (src, dst) in enumerate(tables):
            remote(src, dst.at[z], table_send.at[n, far], table_recv.at[n, z], base + far).start()
    send_slots(0)
    for d in range(1, GROUP):
        far = lax.rem(z + d, GROUP)
        remote(ocean.at[far], state.at[z], state_send.at[far], state_recv.at[z], base + far).start()
    for copy in own[3:]:
        copy.wait()

    def build(i):
        rows = [coeff[i, n : n + 1, :] for n in range(near.shape[1])]
        ids = [near[i, n : n + 1, :] for n in range(near.shape[1])]
        summed = []
        for n in range(len(rows)):
            value = rows[n]
            for m in range(n):
                value = value + jnp.where(ids[m] == ids[n], rows[m], 0.0)
            summed.append(value)
        whole = rows[0]
        for n in range(1, len(rows)):
            whole = whole + rows[n]
        keep[i] = (1.0 - 2.0 * vertical_mix) - whole
        step = 32

        def fill(c, _):
            first = pl.multiple_of(c * step, step)
            for q in range(cells // LANES):
                cols = slice(q * LANES, (q + 1) * LANES)
                place = lax.broadcasted_iota(jnp.int32, (step, LANES), 0) + first
                value = jnp.zeros((step, LANES), F32)
                for n in range(len(rows)):
                    value = jnp.where(ids[n][:, cols] == place, summed[n][:, cols], value)
                high, low = split(value)
                wide_hi[i, pl.ds(first, step), cols] = high
                wide_lo[i, pl.ds(first, step), cols] = low
            return 0

        lax.fori_loop(0, (cells + 2 * rim) // step, fill, 0)

        def select(c, _):
            first = pl.multiple_of(c * step, step)
            place = lax.broadcasted_iota(jnp.int32, (step, rim), 0) + first
            for side in range(2):
                hit = halo[i, side : side + 1, :] == place
                rims[i, pl.ds(first, step), side * rim : (side + 1) * rim] = jnp.where(
                    hit, 1.0, 0.0
                ).astype(BF16)
            return 0

        lax.fori_loop(0, cells // step, select, 0)
        place = lax.broadcasted_iota(jnp.int32, (LANES, cells), 0)
        for k in range(slots.shape[1]):
            hit = (slots[i, k : k + 1, :] & (LANES - 1)) == place
            slot_lanes[i, k] = jnp.where(hit, 1.0, 0.0).astype(BF16)

    def build_all(d, _):
        i = lax.rem(z + d, GROUP)

        @pl.when(d > 0)
        def _():
            for n, (src, dst) in enumerate(tables):
                copy = remote(src, dst.at[i], table_send.at[n, i], table_recv.at[n, i], base + i)
                copy.wait_recv()
                copy.wait_send()

        build(i)
        return 0

    lax.fori_loop(0, GROUP, build_all, 0)

    place = lax.broadcasted_iota(jnp.int32, (LANES, cells), 0)
    for h in range(sends.shape[1] // cells):
        hit = (sends[:, h * cells : (h + 1) * cells] & (LANES - 1)) == place
        point_lanes[:, h * cells : (h + 1) * cells] = jnp.where(hit, 1.0, 0.0).astype(BF16)

    own[2].wait()
    set_parts(z, state[z])
    for d in range(1, GROUP):
        far = lax.rem(z + d, GROUP)
        copy = remote(
            ocean.at[far], state.at[far], state_send.at[far], state_recv.at[far], base + far
        )
        copy.wait_recv()
        copy.wait_send()
        set_parts(far, state[far])
    for i in (0, 3, 1, 2):
        rims_of(0, i)

    def settle(i, value):
        state[i] = value
        set_parts(i, value)

    def first(interval):
        t = STEPS * interval
        if interval:
            for i in range(GROUP):
                slot_sums(0, i)
            sums_out(0)
        early[0] = mixed(0)
        early[1] = mixed(3)
        for i in (1, 2):
            state[i] = mixed(i)
        if interval:
            collect(0)
            gather(1)
            send_slots(1)
        state[0] = rim_arrives(t, 0)
        state[3] = rim_arrives(t, 1)
        rims_sent(t)
        receive_forcing(interval)
        for i in (0, 3, 1, 2):
            settle(i, state[i] + push(i))
            rims_of(t + 1, i)

    def plain(t):
        for i in (1, 2):
            settle(i, mixed(i) + push(i))
        early[0] = mixed(0) + push(0)
        early[1] = mixed(3) + push(3)
        settle(0, rim_arrives(t, 0))
        rims_of(t + 1, 0)
        settle(3, rim_arrives(t, 1))
        rims_of(t + 1, 3)
        rims_of(t + 1, 1)
        rims_of(t + 1, 2)
        rims_sent(t)

    def plain_step(t, _):
        plain(t)
        return 0

    def ship(i):
        @pl.when(z == i)
        def _():
            pltpu.make_async_copy(state.at[i], out_state.at[i], local.at[14]).start()

        @pl.when(z != i)
        def _():
            remote(
                state.at[i], out_state.at[z], out_send.at[i], out_recv.at[z], base + i
            ).start()

    first(0)
    lax.fori_loop(1, STEPS, plain_step, 0)
    first(1)
    plain(STEPS + 1)
    last = 2 * STEPS - 1
    for i in (1, 2):
        state[i] = mixed(i) + push(i)
        ship(i)
    early[0] = mixed(0) + push(0)
    early[1] = mixed(3) + push(3)
    for i in (1, 2):
        slot_sums(1, i)
    state[0] = rim_arrives(last, 0)
    slot_sums(1, 0)
    state[3] = rim_arrives(last, 1)
    slot_sums(1, 3)
    sums_out(1)
    ship(0)
    ship(3)
    rims_sent(last)
    collect(1)
    out_atm[...] = returned[...]
    pltpu.make_async_copy(state.at[z], out_state.at[z], local.at[14]).wait()
    for d in range(1, GROUP):
        far = lax.rem(z + d, GROUP)
        copy = remote(
            state.at[far], out_state.at[far], out_send.at[far], out_recv.at[far], base + far
        )
        copy.wait_recv()
        copy.wait_send()


def shards(
    ocean_state, atm_flux, edge_coeff, neighbours, halo_send, send_idx, recv_slot, regrid_weight
):
    fields, levels, cells = ocean_state.shape
    points = atm_flux.shape[2]
    rim = halo_send.shape[1]
    slot_count = send_idx.shape[1]
    near = neighbours.shape[0]
    sources = recv_slot.shape[0]
    wide = cells + 2 * rim
    steps = 2 * STEPS
    dma = pltpu.SemaphoreType.DMA
    final, atm = pl.pallas_call(
        kernel,
        out_shape=(
            jax.ShapeDtypeStruct((fields, levels, cells), F32),
            jax.ShapeDtypeStruct((fields * points // LANES, LANES), F32),
        ),
        in_specs=[pl.BlockSpec(memory_space=pl.ANY)] * 8,
        out_specs=(
            pl.BlockSpec(memory_space=pl.ANY),
            pl.BlockSpec(memory_space=pltpu.VMEM),
        ),
        scratch_shapes=[
            pltpu.VMEM((GROUP, levels, cells), F32),
            pltpu.VMEM((GROUP, 2 * levels, wide), BF16),
            pltpu.VMEM((GROUP, wide, cells), BF16),
            pltpu.VMEM((GROUP, wide, cells), BF16),
            pltpu.VMEM((GROUP, cells, 2 * rim), BF16),
            pltpu.VMEM((GROUP, near, cells), F32),
            pltpu.VMEM((GROUP, near, cells), jnp.int32),
            pltpu.VMEM((GROUP, 2, rim), jnp.int32),
            pltpu.VMEM((GROUP, sources, cells), jnp.int32),
            pltpu.VMEM((GROUP, sources, cells), F32),
            pltpu.VMEM((1, slot_count), jnp.int32),
            pltpu.VMEM((2, fields, points), F32),
            pltpu.VMEM((PEERS, LANES), jnp.int32),
            pltpu.VMEM((GROUP, 1, cells), F32),
            pltpu.VMEM((levels, cells), F32),
            pltpu.VMEM((GROUP, 1, cells), F32),
            pltpu.VMEM((GROUP, sources, LANES, cells), BF16),
            pltpu.VMEM((LANES, slot_count), BF16),
            pltpu.VMEM((2, fields, 3, GROUP, LANES), F32),
            pltpu.VMEM((2, 3 * GROUP, GROUP, LANES), F32),
            pltpu.VMEM((2, 3 * GROUP, GROUP, 1, LANES), F32),
            pltpu.VMEM((2, 3 * GROUP, GROUP, 1, LANES), F32),
            pltpu.VMEM((fields * points // LANES, LANES), F32),
            pltpu.VMEM((steps, 2, levels, rim), F32),
            pltpu.VMEM((steps, 2, levels, rim), F32),
            pltpu.VMEM((2, levels, cells), F32),
            dma((GROUP,)),
            dma((GROUP,)),
            dma((5, GROUP)),
            dma((5, GROUP)),
            dma((2, 3 * GROUP)),
            dma((2, 3 * GROUP)),
            dma((2, 3 * GROUP)),
            dma((2, 3 * GROUP)),
            dma((steps, 2)),
            dma((steps, 2)),
            dma((GROUP,)),
            dma((GROUP,)),
            dma((15,)),
        ],
        compiler_params=pltpu.CompilerParams(
            collective_id=0, has_side_effects=True, vmem_limit_bytes=67_043_328
        ),
        name="coupled",
    )(
        ocean_state, atm_flux, edge_coeff, neighbours, halo_send, send_idx, recv_slot,
        regrid_weight,
    )
    return final, atm.reshape(fields, points)


def solution(mesh):
    placed = (
        P(None, None, AXES),
        P(None, None, AXES),
        P(None, AXES),
        P(None, AXES),
        P(None, AXES),
        P(AXES, None),
        P(None, AXES),
        P(None, AXES),
    )
    return jax.shard_map(
        shards,
        mesh=mesh,
        in_specs=placed,
        out_specs=(P(None, None, AXES), P(None, AXES)),
        check_vma=False,
    )
```

```python
import jax
import jax.numpy as jnp
from jax import lax
from jax.experimental import pallas as pl
from jax.experimental.pallas import tpu as pltpu
from jax.sharding import PartitionSpec as P

AXES = ("comp", "dom")
MESH = pl.DeviceIdType.MESH
F32 = jnp.float32
BF16 = jnp.bfloat16

PEERS = 8
REACH = 3
STEPS = 3
GROUP = 4
LANES = 128
PIECES = ((0, 48), (48, 80))

vertical_mix = 0.2
forcing_scale = 0.1
relaxation = 0.25
penetration = 8.0


def split(value):
    high = value.astype(BF16)
    return high, (value - high.astype(F32)).astype(BF16)


def across(left, right):
    return lax.dot_general(left, right, (((1,), (1,)), ((), ())), preferred_element_type=F32)


def lookup(table, index):
    return jnp.take_along_axis(table, index, axis=1, mode="promise_in_bounds")


def kernel(
    ocean, flux, coeff_in, near_in, halo_in, send_in, slot_in, weight_in,
    out_state, out_atm,
    state, parts, wide_hi, wide_lo, rims, coeff, near, halo, slots, weights,
    sends, air, sends8, keep, profile, added,
    slot_lanes, point_lanes, outgoing, arrived, sums, back, returned,
    rim_out, rim_in, early,
    state_send, state_recv, table_send, table_recv, flux_send, flux_recv,
    back_send, back_recv, rim_send, rim_recv, out_send, out_recv, local,
):
    levels, cells = state.shape[1:]
    rim = halo.shape[2]
    points = air.shape[2]
    fields = GROUP
    blocks = points // LANES
    doms = lax.axis_size("dom")
    total = lax.axis_size("comp") * doms
    me = lax.axis_index("comp") * doms + lax.axis_index("dom")
    z = lax.rem(me, GROUP)
    base = me - z

    def device(p):
        p = lax.rem(p + total, total)
        return (lax.div(p, doms), lax.rem(p, doms))

    def remote(src, dst, send, recv, p):
        return pltpu.make_async_remote_copy(
            src_ref=src, dst_ref=dst, send_sem=send, recv_sem=recv,
            device_id=device(p), device_id_type=MESH,
        )

    barrier = pltpu.get_barrier_semaphore()
    for r in range(3):
        for k in range(GROUP):
            if r == 1 and k == 0:
                continue
            far = base + GROUP * (r - 1) + lax.rem(z + k, GROUP)
            pl.semaphore_signal(barrier, inc=1, device_id=device(far), device_id_type=MESH)

    tables = [(coeff_in, coeff), (near_in, near), (halo_in, halo), (slot_in, slots), (weight_in, weights)]
    own = [
        pltpu.make_async_copy(send_in, sends, local.at[0]),
        pltpu.make_async_copy(flux, air, local.at[1]),
        pltpu.make_async_copy(ocean.at[z], state.at[z], local.at[2]),
    ] + [
        pltpu.make_async_copy(src, dst.at[z], local.at[3 + n])
        for n, (src, dst) in enumerate(tables)
    ]
    for copy in own:
        copy.start()

    def gather(interval):
        low = sends8[...] & (LANES - 1)
        high = lax.shift_right_logical(sends8[...], 7)
        for f in range(fields):
            total_f = jnp.zeros((PEERS, LANES), F32)
            for b in range(blocks):
                row = air[interval, f : f + 1, b * LANES : (b + 1) * LANES]
                if interval:
                    at = f * blocks + b
                    row = row - relaxation * returned[at : at + 1, :]
                table = jnp.broadcast_to(row, (PEERS, LANES))
                total_f = jnp.where(high == b, lookup(table, low), total_f)
            moved = pltpu.roll(
                jnp.concatenate([total_f, jnp.zeros((PEERS, LANES), F32)], axis=0), z + 1, 0
            )
            for r in range(3):
                outgoing[interval, f, r] = moved[GROUP * r : GROUP * (r + 1), :]

    def send_slots(interval):
        for r in range(3):
            for k in range(GROUP):
                f = lax.rem(z + k, GROUP)
                src = outgoing.at[interval, f, r]
                dst = arrived.at[interval, GROUP * (2 - r) + z]
                if r == 1 and k == 0:
                    pltpu.make_async_copy(src, dst, local.at[8 + interval]).start()
                else:
                    remote(
                        src, dst, flux_send.at[interval, GROUP * r + f],
                        flux_recv.at[interval, GROUP * (2 - r) + z],
                        base + GROUP * (r - 1) + f,
                    ).start()

    def receive_forcing(interval):
        for r in range(3):
            for k in range(GROUP):
                f = lax.rem(z + k, GROUP)
                src = outgoing.at[interval, f, r]
                dst = arrived.at[interval, GROUP * r + f]
                if r == 1 and k == 0:
                    pltpu.make_async_copy(src, dst, local.at[8 + interval]).wait()
                else:
                    copy = remote(
                        src, dst, flux_send.at[interval, GROUP * r + f],
                        flux_recv.at[interval, GROUP * r + f], base + GROUP * (r - 1) + f,
                    )
                    copy.wait_recv()
                    copy.wait_send()
        for i in range(GROUP):
            for pair in range(cells // (2 * LANES)):
                cols = [slice((2 * pair + h) * LANES, (2 * pair + h + 1) * LANES) for h in range(2)]
                index = jnp.concatenate([slots[i, :, c] for c in cols], axis=0)
                weight = jnp.concatenate([weights[i, :, c] for c in cols], axis=0)
                low = index & (LANES - 1)
                high = lax.shift_right_logical(index, 7)
                value = jnp.zeros((PEERS, LANES), F32)
                for j in range(PEERS):
                    row = arrived[interval, 7 + i - j, i : i + 1, :]
                    table = jnp.broadcast_to(row, (PEERS, LANES))
                    value = jnp.where(high == j, lookup(table, low), value)
                value = value * weight
                for h in range(2):
                    added[i, :, cols[h]] = jnp.sum(value[4 * h : 4 * h + 4], axis=0, keepdims=True)

    def slot_sums(interval, i):
        place = lax.broadcasted_iota(jnp.int32, (PEERS, cells), 0)
        acc = jnp.zeros((2 * PEERS, LANES), F32)
        top = state[i, 0:1, :]
        for k in range(slots.shape[1]):
            hit = lax.shift_right_logical(slots[i, k : k + 1, :], 7) == place
            high, low = split(jnp.where(hit, weights[i, k : k + 1, :] * top, 0.0))
            acc = acc + across(jnp.concatenate([high, low], axis=0), slot_lanes[i, k])
        acc = acc[:PEERS] + acc[PEERS:]
        for j in range(PEERS):
            sums[interval, i - j + REACH + GROUP, i] = acc[j : j + 1, :]

    def back_copy(interval, r, k, start):
        f = lax.rem(z + k, GROUP)
        src = sums.at[interval, GROUP * r + f]
        if r == 1 and k == 0:
            dst = back.at[interval, GROUP + z]
            copy = pltpu.make_async_copy(src, dst, local.at[10 + interval])
            copy.start() if start else copy.wait()
            return
        send = back_send.at[interval, GROUP * r + f]
        p = base + GROUP * (r - 1) + f
        slot = GROUP * (2 - r) + z if start else GROUP * r + f
        copy = remote(src, back.at[interval, slot], send, back_recv.at[interval, slot], p)
        if start:
            copy.start()
        else:
            copy.wait_recv()
            copy.wait_send()

    def sums_out(interval):
        for r in range(3):
            for k in range(GROUP):
                back_copy(interval, r, k, True)

    def collect(interval):
        for r in range(3):
            for k in range(GROUP):
                back_copy(interval, r, k, False)
        place = lax.broadcasted_iota(jnp.int32, (blocks, LANES), 0)
        values = []
        for f in range(fields):
            rows = [back[interval, GROUP * r + f, i] for r in range(3) for i in range(GROUP)]
            rows.append(jnp.zeros((GROUP, LANES), F32))
            values.append(pltpu.roll(jnp.concatenate(rows, axis=0), 2 * PEERS - 1 - z, 0))
        columns = []
        for j in range(PEERS):
            hit = lax.shift_right_logical(sends[:, j * LANES : (j + 1) * LANES], 7) == place
            columns.append(
                jnp.concatenate(
                    [jnp.where(hit, values[f][j : j + 1, :], 0.0) for f in range(fields)], axis=0
                )
            )
        high, low = split(jnp.concatenate(columns, axis=1))
        both = across(jnp.concatenate([high, low], axis=0), point_lanes[...])
        returned[...] = both[: fields * blocks] + both[fields * blocks :]

    def set_parts(i, value):
        high, low = split(value)
        parts[i, 0:levels, 0:cells] = high
        parts[i, levels : 2 * levels, 0:cells] = low

    def rim_copy(t, side, c):
        a, b = PIECES[c]
        return remote(
            rim_out.at[t, side, a:b], rim_in.at[t, 1 - side, a:b], rim_send.at[t, side, c],
            rim_recv.at[t, 1 - side, c], me + (GROUP if side else -GROUP),
        )

    def outer_rims(t, side, c):
        i = side * (GROUP - 1)
        a, b = PIECES[c]
        both = jnp.concatenate(
            [parts[i, a:b, 0:cells], parts[i, levels + a : levels + b, 0:cells]], axis=0
        )
        edge = jnp.dot(
            both, rims[i, :, side * rim : (side + 1) * rim], preferred_element_type=F32
        )
        rim_out[t, side, a:b] = edge[0 : b - a] + edge[b - a :]
        rim_copy(t, side, c).start()

    def inner_rims(i):
        for side in range(2):
            j = i - 1 + 2 * side
            if 0 <= j < GROUP:
                edge = jnp.dot(
                    parts[i, :, 0:cells], rims[i, :, side * rim : (side + 1) * rim],
                    preferred_element_type=F32,
                )
                start = cells if side else cells + rim
                parts[j, :, start : start + rim] = edge.astype(BF16)

    def rim_arrives(t, side, c):
        a, b = PIECES[c]
        p = me + (GROUP if side else -GROUP)
        copy = remote(
            rim_out.at[t, 1 - side, a:b], rim_in.at[t, side, a:b], rim_send.at[t, 1 - side, c],
            rim_recv.at[t, side, c], p,
        )
        copy.wait_recv()
        high, low = split(rim_in[t, side, a:b])
        i, start = (GROUP - 1, cells + rim) if side else (0, cells)
        both = jnp.dot(
            jnp.concatenate([high, low], axis=0), wide_hi[i, start : start + rim, :],
            preferred_element_type=F32,
        )
        small = jnp.dot(high, wide_lo[i, start : start + rim, :], preferred_element_type=F32)
        return early[side, a:b] + (both[0 : b - a] + both[b - a :] + small)

    def rims_sent(t):
        for side in range(2):
            for c in range(len(PIECES)):
                rim_copy(t, side, c).wait_send()

    def product(i, first, last):
        both = jnp.dot(
            parts[i, :, first:last], wide_hi[i, first:last, :], preferred_element_type=F32
        )
        small = jnp.dot(
            parts[i, 0:levels, first:last], wide_lo[i, first:last, :], preferred_element_type=F32
        )
        return both[0:levels] + both[levels:] + small

    def mixed(i):
        here = state[i]
        row = lax.broadcasted_iota(jnp.int32, (levels, cells), 0)
        above = jnp.where(row == 0, here, pltpu.roll(here, 1, 0))
        below = jnp.where(row == levels - 1, here, pltpu.roll(here, levels - 1, 0))
        value = keep[i] * here + vertical_mix * (above + below)
        if i == 0:
            return value + product(i, 0, cells) + product(i, cells + rim, cells + 2 * rim)
        if i == GROUP - 1:
            return value + product(i, 0, cells + rim)
        return value + product(i, 0, cells + 2 * rim)

    def push(i):
        return added[i] * profile[...]

    sums[...] = jnp.zeros_like(sums)
    level = lax.broadcasted_iota(jnp.int32, (levels, cells), 0).astype(F32)
    profile[...] = forcing_scale * jnp.exp(-level / penetration)
    own[0].wait()
    own[1].wait()
    sends8[...] = jnp.concatenate(
        [sends[:, j * LANES : (j + 1) * LANES] for j in range(PEERS)], axis=0
    )
    gather(0)
    pl.semaphore_wait(barrier, 3 * GROUP - 1)
    for d in range(1, GROUP):
        far = lax.rem(z + d, GROUP)
        for n, (src, dst) in enumerate(tables):
            remote(src, dst.at[z], table_send.at[n, far], table_recv.at[n, z], base + far).start()
    send_slots(0)
    for d in range(1, GROUP):
        far = lax.rem(z + d, GROUP)
        remote(ocean.at[far], state.at[z], state_send.at[far], state_recv.at[z], base + far).start()
    for copy in own[3:]:
        copy.wait()

    def build(i):
        rows = [coeff[i, n : n + 1, :] for n in range(near.shape[1])]
        ids = [near[i, n : n + 1, :] for n in range(near.shape[1])]
        summed = []
        for n in range(len(rows)):
            value = rows[n]
            for m in range(n):
                value = value + jnp.where(ids[m] == ids[n], rows[m], 0.0)
            summed.append(value)
        whole = rows[0]
        for n in range(1, len(rows)):
            whole = whole + rows[n]
        keep[i] = (1.0 - 2.0 * vertical_mix) - whole
        step = 32

        def fill(c, _):
            first = pl.multiple_of(c * step, step)
            for q in range(cells // LANES):
                cols = slice(q * LANES, (q + 1) * LANES)
                place = lax.broadcasted_iota(jnp.int32, (step, LANES), 0) + first
                value = jnp.zeros((step, LANES), F32)
                for n in range(len(rows)):
                    value = jnp.where(ids[n][:, cols] == place, summed[n][:, cols], value)
                high, low = split(value)
                wide_hi[i, pl.ds(first, step), cols] = high
                wide_lo[i, pl.ds(first, step), cols] = low
            return 0

        lax.fori_loop(0, (cells + 2 * rim) // step, fill, 0)

        def select(c, _):
            first = pl.multiple_of(c * step, step)
            place = lax.broadcasted_iota(jnp.int32, (step, rim), 0) + first
            for side in range(2):
                hit = halo[i, side : side + 1, :] == place
                rims[i, pl.ds(first, step), side * rim : (side + 1) * rim] = jnp.where(
                    hit, 1.0, 0.0
                ).astype(BF16)
            return 0

        lax.fori_loop(0, cells // step, select, 0)
        place = lax.broadcasted_iota(jnp.int32, (LANES, cells), 0)
        for k in range(slots.shape[1]):
            hit = (slots[i, k : k + 1, :] & (LANES - 1)) == place
            slot_lanes[i, k] = jnp.where(hit, 1.0, 0.0).astype(BF16)

    def build_all(d, _):
        i = lax.rem(z + d, GROUP)

        @pl.when(d > 0)
        def _():
            for n, (src, dst) in enumerate(tables):
                copy = remote(src, dst.at[i], table_send.at[n, i], table_recv.at[n, i], base + i)
                copy.wait_recv()
                copy.wait_send()

        build(i)
        return 0

    lax.fori_loop(0, GROUP, build_all, 0)

    place = lax.broadcasted_iota(jnp.int32, (LANES, cells), 0)
    for h in range(sends.shape[1] // cells):
        hit = (sends[:, h * cells : (h + 1) * cells] & (LANES - 1)) == place
        point_lanes[:, h * cells : (h + 1) * cells] = jnp.where(hit, 1.0, 0.0).astype(BF16)

    own[2].wait()
    set_parts(z, state[z])
    for d in range(1, GROUP):
        far = lax.rem(z + d, GROUP)
        copy = remote(
            ocean.at[far], state.at[far], state_send.at[far], state_recv.at[far], base + far
        )
        copy.wait_recv()
        copy.wait_send()
        set_parts(far, state[far])
    pieces = range(len(PIECES))

    def all_rims(t):
        for c in pieces:
            outer_rims(t, 0, c)
            outer_rims(t, 1, c)
        for i in (0, 3, 1, 2):
            inner_rims(i)

    all_rims(0)

    def settle(i, value):
        state[i] = value
        set_parts(i, value)

    def settle_piece(i, c, value):
        a, b = PIECES[c]
        high, low = split(value)
        state[i, a:b] = value
        parts[i, a:b, 0:cells] = high
        parts[i, levels + a : levels + b, 0:cells] = low

    def first(interval):
        t = STEPS * interval
        if interval:
            for i in range(GROUP):
                slot_sums(0, i)
            sums_out(0)
        early[0] = mixed(0)
        early[1] = mixed(3)
        for i in (1, 2):
            state[i] = mixed(i)
        if interval:
            collect(0)
            gather(1)
            send_slots(1)
        for c in pieces:
            a, b = PIECES[c]
            state[0, a:b] = rim_arrives(t, 0, c)
            state[3, a:b] = rim_arrives(t, 1, c)
        rims_sent(t)
        receive_forcing(interval)
        for i in (0, 3, 1, 2):
            settle(i, state[i] + push(i))
        all_rims(t + 1)

    def plain(t):
        for i in (1, 2):
            settle(i, mixed(i) + push(i))
        early[0] = mixed(0) + push(0)
        early[1] = mixed(3) + push(3)
        for c in pieces:
            for side in range(2):
                settle_piece(side * (GROUP - 1), c, rim_arrives(t, side, c))
                outer_rims(t + 1, side, c)
        for i in (0, 3, 1, 2):
            inner_rims(i)
        rims_sent(t)

    def plain_step(t, _):
        plain(t)
        return 0

    def ship(i):
        @pl.when(z == i)
        def _():
            pltpu.make_async_copy(state.at[i], out_state.at[i], local.at[14]).start()

        @pl.when(z != i)
        def _():
            remote(
                state.at[i], out_state.at[z], out_send.at[i], out_recv.at[z], base + i
            ).start()

    first(0)
    lax.fori_loop(1, STEPS, plain_step, 0)
    first(1)
    plain(STEPS + 1)
    last = 2 * STEPS - 1
    for i in (1, 2):
        state[i] = mixed(i) + push(i)
        ship(i)
    early[0] = mixed(0) + push(0)
    early[1] = mixed(3) + push(3)
    for i in (1, 2):
        slot_sums(1, i)
    for c in pieces:
        a, b = PIECES[c]
        state[0, a:b] = rim_arrives(last, 0, c)
        state[3, a:b] = rim_arrives(last, 1, c)
        if c == 0:
            slot_sums(1, 0)
            slot_sums(1, 3)
            sums_out(1)
    ship(0)
    ship(3)
    rims_sent(last)
    collect(1)
    for b in range(blocks):
        out_atm[:, b * LANES : (b + 1) * LANES] = jnp.concatenate(
            [returned[f * blocks + b : f * blocks + b + 1, :] for f in range(fields)], axis=0
        )
    pltpu.make_async_copy(state.at[z], out_state.at[z], local.at[14]).wait()
    for d in range(1, GROUP):
        far = lax.rem(z + d, GROUP)
        copy = remote(
            state.at[far], out_state.at[far], out_send.at[far], out_recv.at[far], base + far
        )
        copy.wait_recv()
        copy.wait_send()


def shards(
    ocean_state, atm_flux, edge_coeff, neighbours, halo_send, send_idx, recv_slot, regrid_weight
):
    fields, levels, cells = ocean_state.shape
    points = atm_flux.shape[2]
    rim = halo_send.shape[1]
    slot_count = send_idx.shape[1]
    near = neighbours.shape[0]
    sources = recv_slot.shape[0]
    wide = cells + 2 * rim
    steps = 2 * STEPS
    dma = pltpu.SemaphoreType.DMA
    final, atm = pl.pallas_call(
        kernel,
        out_shape=(
            jax.ShapeDtypeStruct((fields, levels, cells), F32),
            jax.ShapeDtypeStruct((fields, points), F32),
        ),
        in_specs=[pl.BlockSpec(memory_space=pltpu.HBM)] * 8,
        out_specs=(
            pl.BlockSpec(memory_space=pl.ANY),
            pl.BlockSpec(memory_space=pltpu.VMEM),
        ),
        scratch_shapes=[
            pltpu.VMEM((GROUP, levels, cells), F32),
            pltpu.VMEM((GROUP, 2 * levels, wide), BF16),
            pltpu.VMEM((GROUP, wide, cells), BF16),
            pltpu.VMEM((GROUP, wide, cells), BF16),
            pltpu.VMEM((GROUP, cells, 2 * rim), BF16),
            pltpu.VMEM((GROUP, near, cells), F32),
            pltpu.VMEM((GROUP, near, cells), jnp.int32),
            pltpu.VMEM((GROUP, 2, rim), jnp.int32),
            pltpu.VMEM((GROUP, sources, cells), jnp.int32),
            pltpu.VMEM((GROUP, sources, cells), F32),
            pltpu.VMEM((1, slot_count), jnp.int32),
            pltpu.VMEM((2, fields, points), F32),
            pltpu.VMEM((PEERS, LANES), jnp.int32),
            pltpu.VMEM((GROUP, 1, cells), F32),
            pltpu.VMEM((levels, cells), F32),
            pltpu.VMEM((GROUP, 1, cells), F32),
            pltpu.VMEM((GROUP, sources, LANES, cells), BF16),
            pltpu.VMEM((LANES, slot_count), BF16),
            pltpu.VMEM((2, fields, 3, GROUP, LANES), F32),
            pltpu.VMEM((2, 3 * GROUP, GROUP, LANES), F32),
            pltpu.VMEM((2, 3 * GROUP, GROUP, 1, LANES), F32),
            pltpu.VMEM((2, 3 * GROUP, GROUP, 1, LANES), F32),
            pltpu.VMEM((fields * points // LANES, LANES), F32),
            pltpu.VMEM((steps, 2, levels, rim), F32),
            pltpu.VMEM((steps, 2, levels, rim), F32),
            pltpu.VMEM((2, levels, cells), F32),
            dma((GROUP,)),
            dma((GROUP,)),
            dma((5, GROUP)),
            dma((5, GROUP)),
            dma((2, 3 * GROUP)),
            dma((2, 3 * GROUP)),
            dma((2, 3 * GROUP)),
            dma((2, 3 * GROUP)),
            dma((steps, 2, len(PIECES))),
            dma((steps, 2, len(PIECES))),
            dma((GROUP,)),
            dma((GROUP,)),
            dma((15,)),
        ],
        compiler_params=pltpu.CompilerParams(
            collective_id=0, has_side_effects=True, vmem_limit_bytes=67_043_328
        ),
        name="coupled",
    )(
        ocean_state, atm_flux, edge_coeff, neighbours, halo_send, send_idx, recv_slot,
        regrid_weight,
    )
    return final, atm


def solution(mesh):
    placed = (
        P(None, None, AXES),
        P(None, None, AXES),
        P(None, AXES),
        P(None, AXES),
        P(None, AXES),
        P(AXES, None),
        P(None, AXES),
        P(None, AXES),
    )
    return jax.shard_map(
        shards,
        mesh=mesh,
        in_specs=placed,
        out_specs=(P(None, None, AXES), P(None, AXES)),
        check_vma=False,
    )
```

```python
import jax
import jax.numpy as jnp
from jax import lax
from jax.experimental import pallas as pl
from jax.experimental.pallas import tpu as pltpu
from jax.sharding import PartitionSpec as P

AXES = ("comp", "dom")
MESH = pl.DeviceIdType.MESH
F32 = jnp.float32
BF16 = jnp.bfloat16

PEERS = 8
REACH = 3
STEPS = 3
GROUP = 4
LANES = 128
PIECES = ((0, 48), (48, 80))

vertical_mix = 0.2
forcing_scale = 0.1
relaxation = 0.25
penetration = 8.0


def split(value):
    high = value.astype(BF16)
    return high, (value - high.astype(F32)).astype(BF16)


def across(left, right):
    return lax.dot_general(left, right, (((1,), (1,)), ((), ())), preferred_element_type=F32)


def lookup(table, index):
    return jnp.take_along_axis(table, index, axis=1, mode="promise_in_bounds")


def kernel(
    ocean, flux, coeff_in, near_in, halo_in, send_in, slot_in, weight_in,
    out_state, out_atm,
    state, parts, wide_hi, wide_lo, rims, coeff, near, halo, slots, weights,
    sends, air, sends8, keep, profile, added,
    slot_lanes, point_lanes, outgoing, arrived, sums, back, returned,
    rim_out, rim_in, early, owner_state, owner_rims,
    state_send, state_recv, table_send, table_recv, flux_send, flux_recv,
    back_send, back_recv, rim_send, rim_recv, owner_send, out_send, out_recv, local,
):
    levels, cells = state.shape[1:]
    rim = halo.shape[2]
    points = air.shape[2]
    fields = GROUP
    blocks = points // LANES
    doms = lax.axis_size("dom")
    total = lax.axis_size("comp") * doms
    me = lax.axis_index("comp") * doms + lax.axis_index("dom")
    z = lax.rem(me, GROUP)
    base = me - z

    def device(p):
        p = lax.rem(p + total, total)
        return (lax.div(p, doms), lax.rem(p, doms))

    def remote(src, dst, send, recv, p):
        return pltpu.make_async_remote_copy(
            src_ref=src, dst_ref=dst, send_sem=send, recv_sem=recv,
            device_id=device(p), device_id_type=MESH,
        )

    barrier = pltpu.get_barrier_semaphore()
    for r in range(3):
        for k in range(GROUP):
            if r == 1 and k == 0:
                continue
            far = base + GROUP * (r - 1) + lax.rem(z + k, GROUP)
            pl.semaphore_signal(barrier, inc=1, device_id=device(far), device_id_type=MESH)

    tables = [(coeff_in, coeff), (near_in, near), (halo_in, halo), (slot_in, slots), (weight_in, weights)]
    own = [
        pltpu.make_async_copy(send_in, sends, local.at[0]),
        pltpu.make_async_copy(flux, air, local.at[1]),
        pltpu.make_async_copy(ocean.at[z], state.at[z], local.at[2]),
    ] + [
        pltpu.make_async_copy(src, dst.at[z], local.at[3 + n])
        for n, (src, dst) in enumerate(tables)
    ] + [pltpu.make_async_copy(ocean, owner_state, local.at[15])]
    for copy in own:
        copy.start()

    def gather(interval):
        low = sends8[...] & (LANES - 1)
        high = lax.shift_right_logical(sends8[...], 7)
        for f in range(fields):
            total_f = jnp.zeros((PEERS, LANES), F32)
            for b in range(blocks):
                row = air[interval, f : f + 1, b * LANES : (b + 1) * LANES]
                if interval:
                    at = f * blocks + b
                    row = row - relaxation * returned[at : at + 1, :]
                table = jnp.broadcast_to(row, (PEERS, LANES))
                total_f = jnp.where(high == b, lookup(table, low), total_f)
            moved = pltpu.roll(
                jnp.concatenate([total_f, jnp.zeros((PEERS, LANES), F32)], axis=0), z + 1, 0
            )
            for r in range(3):
                outgoing[interval, f, r] = moved[GROUP * r : GROUP * (r + 1), :]

    def send_slots(interval):
        for r in range(3):
            for k in range(GROUP):
                f = lax.rem(z + k, GROUP)
                src = outgoing.at[interval, f, r]
                dst = arrived.at[interval, GROUP * (2 - r) + z]
                if r == 1 and k == 0:
                    pltpu.make_async_copy(src, dst, local.at[8 + interval]).start()
                else:
                    remote(
                        src, dst, flux_send.at[interval, GROUP * r + f],
                        flux_recv.at[interval, GROUP * (2 - r) + z],
                        base + GROUP * (r - 1) + f,
                    ).start()

    def receive_forcing(interval):
        for r in range(3):
            for k in range(GROUP):
                f = lax.rem(z + k, GROUP)
                src = outgoing.at[interval, f, r]
                dst = arrived.at[interval, GROUP * r + f]
                if r == 1 and k == 0:
                    pltpu.make_async_copy(src, dst, local.at[8 + interval]).wait()
                else:
                    copy = remote(
                        src, dst, flux_send.at[interval, GROUP * r + f],
                        flux_recv.at[interval, GROUP * r + f], base + GROUP * (r - 1) + f,
                    )
                    copy.wait_recv()
                    copy.wait_send()
    def cell_forcing(interval, i):
        for pair in range(cells // (2 * LANES)):
            cols = [slice((2 * pair + h) * LANES, (2 * pair + h + 1) * LANES) for h in range(2)]
            index = jnp.concatenate([slots[i, :, c] for c in cols], axis=0)
            weight = jnp.concatenate([weights[i, :, c] for c in cols], axis=0)
            low = index & (LANES - 1)
            high = lax.shift_right_logical(index, 7)
            value = jnp.zeros((PEERS, LANES), F32)
            for j in range(PEERS):
                row = arrived[interval, 7 + i - j, i : i + 1, :]
                table = jnp.broadcast_to(row, (PEERS, LANES))
                value = jnp.where(high == j, lookup(table, low), value)
            value = value * weight
            for h in range(2):
                added[i, :, cols[h]] = jnp.sum(value[4 * h : 4 * h + 4], axis=0, keepdims=True)

    def slot_sums(interval, i):
        place = lax.broadcasted_iota(jnp.int32, (PEERS, cells), 0)
        acc = jnp.zeros((2 * PEERS, LANES), F32)
        top = state[i, 0:1, :]
        for k in range(slots.shape[1]):
            hit = lax.shift_right_logical(slots[i, k : k + 1, :], 7) == place
            high, low = split(jnp.where(hit, weights[i, k : k + 1, :] * top, 0.0))
            acc = acc + across(jnp.concatenate([high, low], axis=0), slot_lanes[i, k])
        acc = acc[:PEERS] + acc[PEERS:]
        for j in range(PEERS):
            sums[interval, i - j + REACH + GROUP, i] = acc[j : j + 1, :]

    def back_copy(interval, r, k, start):
        f = lax.rem(z + k, GROUP)
        src = sums.at[interval, GROUP * r + f]
        if r == 1 and k == 0:
            dst = back.at[interval, GROUP + z]
            copy = pltpu.make_async_copy(src, dst, local.at[10 + interval])
            copy.start() if start else copy.wait()
            return
        send = back_send.at[interval, GROUP * r + f]
        p = base + GROUP * (r - 1) + f
        slot = GROUP * (2 - r) + z if start else GROUP * r + f
        copy = remote(src, back.at[interval, slot], send, back_recv.at[interval, slot], p)
        if start:
            copy.start()
        else:
            copy.wait_recv()
            copy.wait_send()

    def sums_out(interval):
        for r in range(3):
            for k in range(GROUP):
                back_copy(interval, r, k, True)

    def collect(interval):
        for r in range(3):
            for k in range(GROUP):
                back_copy(interval, r, k, False)
        place = lax.broadcasted_iota(jnp.int32, (blocks, LANES), 0)
        values = []
        for f in range(fields):
            rows = [back[interval, GROUP * r + f, i] for r in range(3) for i in range(GROUP)]
            rows.append(jnp.zeros((GROUP, LANES), F32))
            values.append(pltpu.roll(jnp.concatenate(rows, axis=0), 2 * PEERS - 1 - z, 0))
        columns = []
        for j in range(PEERS):
            hit = lax.shift_right_logical(sends[:, j * LANES : (j + 1) * LANES], 7) == place
            columns.append(
                jnp.concatenate(
                    [jnp.where(hit, values[f][j : j + 1, :], 0.0) for f in range(fields)], axis=0
                )
            )
        high, low = split(jnp.concatenate(columns, axis=1))
        both = across(jnp.concatenate([high, low], axis=0), point_lanes[...])
        returned[...] = both[: fields * blocks] + both[fields * blocks :]

    def set_parts(i, value):
        high, low = split(value)
        parts[i, 0:levels, 0:cells] = high
        parts[i, levels : 2 * levels, 0:cells] = low

    def rim_copy(t, side, c):
        a, b = PIECES[c]
        return remote(
            rim_out.at[t, side, a:b], rim_in.at[t, 1 - side, a:b], rim_send.at[t, side, c],
            rim_recv.at[t, 1 - side, c], me + (GROUP if side else -GROUP),
        )

    def outer_rims(t, side, c):
        i = side * (GROUP - 1)
        a, b = PIECES[c]
        both = jnp.concatenate(
            [parts[i, a:b, 0:cells], parts[i, levels + a : levels + b, 0:cells]], axis=0
        )
        edge = jnp.dot(
            both, rims[i, :, side * rim : (side + 1) * rim], preferred_element_type=F32
        )
        rim_out[t, side, a:b] = edge[0 : b - a] + edge[b - a :]
        rim_copy(t, side, c).start()

    def inner_rims(i):
        for side in range(2):
            j = i - 1 + 2 * side
            if 0 <= j < GROUP:
                edge = jnp.dot(
                    parts[i, :, 0:cells], rims[i, :, side * rim : (side + 1) * rim],
                    preferred_element_type=F32,
                )
                start = cells if side else cells + rim
                parts[j, :, start : start + rim] = edge.astype(BF16)

    def rim_arrives(t, side, c):
        a, b = PIECES[c]
        p = me + (GROUP if side else -GROUP)
        copy = remote(
            rim_out.at[t, 1 - side, a:b], rim_in.at[t, side, a:b], rim_send.at[t, 1 - side, c],
            rim_recv.at[t, side, c], p,
        )
        copy.wait_recv()
        high, low = split(rim_in[t, side, a:b])
        i, start = (GROUP - 1, cells + rim) if side else (0, cells)
        both = jnp.dot(
            jnp.concatenate([high, low], axis=0), wide_hi[i, start : start + rim, :],
            preferred_element_type=F32,
        )
        small = jnp.dot(high, wide_lo[i, start : start + rim, :], preferred_element_type=F32)
        return early[side, a:b] + (both[0 : b - a] + both[b - a :] + small)

    def rims_sent(t):
        for side in range(2):
            for c in range(len(PIECES)):
                rim_copy(t, side, c).wait_send()

    def product(i, first, last):
        both = jnp.dot(
            parts[i, :, first:last], wide_hi[i, first:last, :], preferred_element_type=F32
        )
        small = jnp.dot(
            parts[i, 0:levels, first:last], wide_lo[i, first:last, :], preferred_element_type=F32
        )
        return both[0:levels] + both[levels:] + small

    def mixed(i):
        here = state[i]
        row = lax.broadcasted_iota(jnp.int32, (levels, cells), 0)
        above = jnp.where(row == 0, here, pltpu.roll(here, 1, 0))
        below = jnp.where(row == levels - 1, here, pltpu.roll(here, levels - 1, 0))
        value = keep[i] * here + vertical_mix * (above + below)
        if i == 0:
            return value + product(i, 0, cells) + product(i, cells + rim, cells + 2 * rim)
        if i == GROUP - 1:
            return value + product(i, 0, cells + rim)
        return value + product(i, 0, cells + 2 * rim)

    def push(i):
        return added[i] * profile[...]

    sums[...] = jnp.zeros_like(sums)
    level = lax.broadcasted_iota(jnp.int32, (levels, cells), 0).astype(F32)
    profile[...] = forcing_scale * jnp.exp(-level / penetration)
    own[0].wait()
    own[1].wait()
    sends8[...] = jnp.concatenate(
        [sends[:, j * LANES : (j + 1) * LANES] for j in range(PEERS)], axis=0
    )
    gather(0)
    for copy in own[3:]:
        copy.wait()
    step = 32

    def build_rims(i):
        def select(c, _):
            first = pl.multiple_of(c * step, step)
            place = lax.broadcasted_iota(jnp.int32, (step, rim), 0) + first
            for side in range(2):
                hit = halo[i, side : side + 1, :] == place
                rims[i, pl.ds(first, step), side * rim : (side + 1) * rim] = jnp.where(
                    hit, 1.0, 0.0
                ).astype(BF16)
            return 0

        lax.fori_loop(0, cells // step, select, 0)

    build_rims(z)

    def owner_copy(side, f, c):
        a, b = PIECES[c]
        return remote(
            owner_rims.at[f, a:b], rim_in.at[0, 1 - side, a:b], owner_send.at[f, c],
            rim_recv.at[0, 1 - side, c], base + (GROUP if side else -GROUP) + f,
        )

    def at_ends(act):
        for side in range(2):
            @pl.when(z == side * (GROUP - 1))
            def _():
                act(side)

    def first_rims(side):
        for f in range(fields):
            high, low = split(owner_state[f])
            edge = jnp.dot(
                jnp.concatenate([high, low], axis=0),
                rims[z, :, side * rim : (side + 1) * rim],
                preferred_element_type=F32,
            )
            owner_rims[f] = edge[0:levels] + edge[levels:]

    def first_rims_go(side):
        for c in range(len(PIECES)):
            for f in range(fields):
                owner_copy(side, f, c).start()

    def first_rims_sent(side):
        for c in range(len(PIECES)):
            for f in range(fields):
                owner_copy(side, f, c).wait_send()

    at_ends(first_rims)
    pl.semaphore_wait(barrier, 3 * GROUP - 1)
    for d in range(1, GROUP):
        far = lax.rem(z + d, GROUP)
        for n, (src, dst) in enumerate(tables):
            remote(src, dst.at[z], table_send.at[n, far], table_recv.at[n, z], base + far).start()
    send_slots(0)
    for d in range(1, GROUP):
        far = lax.rem(z + d, GROUP)
        remote(ocean.at[far], state.at[z], state_send.at[far], state_recv.at[z], base + far).start()
    at_ends(first_rims_go)

    def build(i):
        rows = [coeff[i, n : n + 1, :] for n in range(near.shape[1])]
        ids = [near[i, n : n + 1, :] for n in range(near.shape[1])]
        summed = []
        for n in range(len(rows)):
            value = rows[n]
            for m in range(n):
                value = value + jnp.where(ids[m] == ids[n], rows[m], 0.0)
            summed.append(value)
        whole = rows[0]
        for n in range(1, len(rows)):
            whole = whole + rows[n]
        keep[i] = (1.0 - 2.0 * vertical_mix) - whole

        def fill(c, _):
            first = pl.multiple_of(c * step, step)
            for q in range(cells // LANES):
                cols = slice(q * LANES, (q + 1) * LANES)
                place = lax.broadcasted_iota(jnp.int32, (step, LANES), 0) + first
                value = jnp.zeros((step, LANES), F32)
                for n in range(len(rows)):
                    value = jnp.where(ids[n][:, cols] == place, summed[n][:, cols], value)
                high, low = split(value)
                wide_hi[i, pl.ds(first, step), cols] = high
                wide_lo[i, pl.ds(first, step), cols] = low
            return 0

        lax.fori_loop(0, (cells + 2 * rim) // step, fill, 0)

        @pl.when(i != z)
        def _():
            build_rims(i)

        place = lax.broadcasted_iota(jnp.int32, (LANES, cells), 0)
        for k in range(slots.shape[1]):
            hit = (slots[i, k : k + 1, :] & (LANES - 1)) == place
            slot_lanes[i, k] = jnp.where(hit, 1.0, 0.0).astype(BF16)

    def build_all(d, _):
        i = lax.rem(z + d, GROUP)

        @pl.when(d > 0)
        def _():
            for n, (src, dst) in enumerate(tables):
                copy = remote(src, dst.at[i], table_send.at[n, i], table_recv.at[n, i], base + i)
                copy.wait_recv()
                copy.wait_send()

        build(i)
        return 0

    lax.fori_loop(0, GROUP, build_all, 0)

    place = lax.broadcasted_iota(jnp.int32, (LANES, cells), 0)
    for h in range(sends.shape[1] // cells):
        hit = (sends[:, h * cells : (h + 1) * cells] & (LANES - 1)) == place
        point_lanes[:, h * cells : (h + 1) * cells] = jnp.where(hit, 1.0, 0.0).astype(BF16)

    own[2].wait()
    set_parts(z, state[z])
    for d in range(1, GROUP):
        far = lax.rem(z + d, GROUP)
        copy = remote(
            ocean.at[far], state.at[far], state_send.at[far], state_recv.at[far], base + far
        )
        copy.wait_recv()
        copy.wait_send()
        set_parts(far, state[far])
    pieces = range(len(PIECES))

    for i in (0, 3, 1, 2):
        inner_rims(i)

    def settle(i, value):
        state[i] = value
        set_parts(i, value)

    def settle_piece(i, c, value):
        a, b = PIECES[c]
        high, low = split(value)
        state[i, a:b] = value
        parts[i, a:b, 0:cells] = high
        parts[i, levels + a : levels + b, 0:cells] = low

    def first(interval):
        t = STEPS * interval
        early[0] = mixed(0)
        early[1] = mixed(3)
        for i in (1, 2):
            state[i] = mixed(i)
        if interval:
            collect(0)
            gather(1)
            send_slots(1)
        for c in pieces:
            a, b = PIECES[c]
            state[0, a:b] = rim_arrives(t, 0, c)
            state[3, a:b] = rim_arrives(t, 1, c)
        receive_forcing(interval)
        for i in (0, 3):
            cell_forcing(interval, i)
            settle(i, state[i] + push(i))
        for c in pieces:
            outer_rims(t + 1, 0, c)
            outer_rims(t + 1, 1, c)
        for i in (1, 2):
            cell_forcing(interval, i)
            settle(i, state[i] + push(i))
        for i in (0, 3, 1, 2):
            inner_rims(i)
        if interval:
            rims_sent(t)
        else:
            at_ends(first_rims_sent)

    def plain(t, sums_too=False):
        for i in (1, 2):
            settle(i, mixed(i) + push(i))
        early[0] = mixed(0) + push(0)
        early[1] = mixed(3) + push(3)
        if sums_too:
            slot_sums(0, 1)
            slot_sums(0, 2)
        for c in pieces:
            for side in range(2):
                settle_piece(side * (GROUP - 1), c, rim_arrives(t, side, c))
                outer_rims(t + 1, side, c)
            if sums_too and c == 0:
                slot_sums(0, 0)
                slot_sums(0, 3)
                sums_out(0)
        for i in (0, 3, 1, 2):
            inner_rims(i)
        rims_sent(t)

    def ship(i):
        @pl.when(z == i)
        def _():
            pltpu.make_async_copy(state.at[i], out_state.at[i], local.at[14]).start()

        @pl.when(z != i)
        def _():
            remote(
                state.at[i], out_state.at[z], out_send.at[i], out_recv.at[z], base + i
            ).start()

    first(0)
    for t in range(1, STEPS):
        plain(t, t == STEPS - 1)
    first(1)
    plain(STEPS + 1)
    last = 2 * STEPS - 1
    for i in (1, 2):
        state[i] = mixed(i) + push(i)
        slot_sums(1, i)
        state[i] = 0.5 * state[i]
        ship(i)
    early[0] = mixed(0) + push(0)
    early[1] = mixed(3) + push(3)
    for c in pieces:
        a, b = PIECES[c]
        state[0, a:b] = rim_arrives(last, 0, c)
        state[3, a:b] = rim_arrives(last, 1, c)
        if c == 0:
            slot_sums(1, 0)
            slot_sums(1, 3)
            sums_out(1)
    for i in (0, 3):
        state[i] = 0.5 * state[i]
        ship(i)
    rims_sent(last)
    collect(1)
    for b in range(blocks):
        out_atm[:, b * LANES : (b + 1) * LANES] = jnp.concatenate(
            [returned[f * blocks + b : f * blocks + b + 1, :] for f in range(fields)], axis=0
        )
    pltpu.make_async_copy(state.at[z], out_state.at[z], local.at[14]).wait()
    for d in range(1, GROUP):
        far = lax.rem(z + d, GROUP)
        copy = remote(
            state.at[far], out_state.at[far], out_send.at[far], out_recv.at[far], base + far
        )
        copy.wait_recv()
        copy.wait_send()


def shards(
    ocean_state, atm_flux, edge_coeff, neighbours, halo_send, send_idx, recv_slot, regrid_weight
):
    fields, levels, cells = ocean_state.shape
    points = atm_flux.shape[2]
    rim = halo_send.shape[1]
    slot_count = send_idx.shape[1]
    near = neighbours.shape[0]
    sources = recv_slot.shape[0]
    wide = cells + 2 * rim
    steps = 2 * STEPS
    dma = pltpu.SemaphoreType.DMA
    final, atm = pl.pallas_call(
        kernel,
        out_shape=(
            jax.ShapeDtypeStruct((fields, levels, cells), F32),
            jax.ShapeDtypeStruct((fields, points), F32),
        ),
        in_specs=[pl.BlockSpec(memory_space=pltpu.HBM)] * 8,
        out_specs=(
            pl.BlockSpec(memory_space=pl.ANY),
            pl.BlockSpec(memory_space=pltpu.VMEM),
        ),
        scratch_shapes=[
            pltpu.VMEM((GROUP, levels, cells), F32),
            pltpu.VMEM((GROUP, 2 * levels, wide), BF16),
            pltpu.VMEM((GROUP, wide, cells), BF16),
            pltpu.VMEM((GROUP, wide, cells), BF16),
            pltpu.VMEM((GROUP, cells, 2 * rim), BF16),
            pltpu.VMEM((GROUP, near, cells), F32),
            pltpu.VMEM((GROUP, near, cells), jnp.int32),
            pltpu.VMEM((GROUP, 2, rim), jnp.int32),
            pltpu.VMEM((GROUP, sources, cells), jnp.int32),
            pltpu.VMEM((GROUP, sources, cells), F32),
            pltpu.VMEM((1, slot_count), jnp.int32),
            pltpu.VMEM((2, fields, points), F32),
            pltpu.VMEM((PEERS, LANES), jnp.int32),
            pltpu.VMEM((GROUP, 1, cells), F32),
            pltpu.VMEM((levels, cells), F32),
            pltpu.VMEM((GROUP, 1, cells), F32),
            pltpu.VMEM((GROUP, sources, LANES, cells), BF16),
            pltpu.VMEM((LANES, slot_count), BF16),
            pltpu.VMEM((2, fields, 3, GROUP, LANES), F32),
            pltpu.VMEM((2, 3 * GROUP, GROUP, LANES), F32),
            pltpu.VMEM((2, 3 * GROUP, GROUP, 1, LANES), F32),
            pltpu.VMEM((2, 3 * GROUP, GROUP, 1, LANES), F32),
            pltpu.VMEM((fields * points // LANES, LANES), F32),
            pltpu.VMEM((steps, 2, levels, rim), F32),
            pltpu.VMEM((steps, 2, levels, rim), F32),
            pltpu.VMEM((2, levels, cells), F32),
            pltpu.VMEM((fields, levels, cells), F32),
            pltpu.VMEM((fields, levels, rim), F32),
            dma((GROUP,)),
            dma((GROUP,)),
            dma((5, GROUP)),
            dma((5, GROUP)),
            dma((2, 3 * GROUP)),
            dma((2, 3 * GROUP)),
            dma((2, 3 * GROUP)),
            dma((2, 3 * GROUP)),
            dma((steps, 2, len(PIECES))),
            dma((steps, 2, len(PIECES))),
            dma((fields, len(PIECES))),
            dma((GROUP,)),
            dma((GROUP,)),
            dma((16,)),
        ],
        compiler_params=pltpu.CompilerParams(
            collective_id=0, has_side_effects=True, vmem_limit_bytes=67_043_328
        ),
        name="coupled",
    )(
        ocean_state, atm_flux, edge_coeff, neighbours, halo_send, send_idx, recv_slot,
        regrid_weight,
    )
    return 2.0 * final, atm


def solution(mesh):
    placed = (
        P(None, None, AXES),
        P(None, None, AXES),
        P(None, AXES),
        P(None, AXES),
        P(None, AXES),
        P(AXES, None),
        P(None, AXES),
        P(None, AXES),
    )
    return jax.shard_map(
        shards,
        mesh=mesh,
        in_specs=placed,
        out_specs=(P(None, None, AXES), P(None, AXES)),
        check_vma=False,
    )
```

```python
import jax
import jax.numpy as jnp
from jax import lax
from jax.experimental import pallas as pl
from jax.experimental.pallas import tpu as pltpu
from jax.sharding import PartitionSpec as P

AXES = ("comp", "dom")
MESH = pl.DeviceIdType.MESH
F32 = jnp.float32
BF16 = jnp.bfloat16

PEERS = 8
REACH = 3
STEPS = 3
GROUP = 4
LANES = 128
PIECES = ((0, 48), (48, 80))

vertical_mix = 0.2
forcing_scale = 0.1
relaxation = 0.25
penetration = 8.0


def split(value):
    high = value.astype(BF16)
    return high, (value - high.astype(F32)).astype(BF16)


def across(left, right):
    return lax.dot_general(left, right, (((1,), (1,)), ((), ())), preferred_element_type=F32)


def lookup(table, index):
    return jnp.take_along_axis(table, index, axis=1, mode="promise_in_bounds")


def kernel(
    ocean, flux, coeff_in, near_in, halo_in, send_in, slot_in, weight_in,
    out_state, out_atm,
    state, parts, wide_hi, wide_lo, rims, coeff, near, halo, slots, weights,
    sends, air, sends8, keep, profile, added,
    slot_lanes, point_lanes, outgoing, arrived, sums, back, returned,
    rim_out, rim_in, early, owner_state, owner_rims,
    state_send, state_recv, table_send, table_recv, flux_send, flux_recv,
    back_send, back_recv, rim_send, rim_recv, owner_send, out_send, out_recv, local,
):
    levels, cells = state.shape[1:]
    rim = halo.shape[2]
    points = air.shape[2]
    fields = GROUP
    blocks = points // LANES
    doms = lax.axis_size("dom")
    total = lax.axis_size("comp") * doms
    me = lax.axis_index("comp") * doms + lax.axis_index("dom")
    z = lax.rem(me, GROUP)
    base = me - z

    def device(p):
        p = lax.rem(p + total, total)
        return (lax.div(p, doms), lax.rem(p, doms))

    def remote(src, dst, send, recv, p):
        return pltpu.make_async_remote_copy(
            src_ref=src, dst_ref=dst, send_sem=send, recv_sem=recv,
            device_id=device(p), device_id_type=MESH,
        )

    barrier = pltpu.get_barrier_semaphore()
    for r in range(3):
        for k in range(GROUP):
            if r == 1 and k == 0:
                continue
            far = base + GROUP * (r - 1) + lax.rem(z + k, GROUP)
            pl.semaphore_signal(barrier, inc=1, device_id=device(far), device_id_type=MESH)

    tables = [(coeff_in, coeff), (near_in, near), (halo_in, halo), (slot_in, slots), (weight_in, weights)]
    own = [
        pltpu.make_async_copy(send_in, sends, local.at[0]),
        pltpu.make_async_copy(flux, air, local.at[1]),
        pltpu.make_async_copy(ocean.at[z], state.at[z], local.at[2]),
    ] + [
        pltpu.make_async_copy(src, dst.at[z], local.at[3 + n])
        for n, (src, dst) in enumerate(tables)
    ] + [pltpu.make_async_copy(ocean, owner_state, local.at[15])]
    for copy in own:
        copy.start()

    def gather(interval):
        low = sends8[...] & (LANES - 1)
        high = lax.shift_right_logical(sends8[...], 7)
        for f in range(fields):
            total_f = jnp.zeros((PEERS, LANES), F32)
            for b in range(blocks):
                row = air[interval, f : f + 1, b * LANES : (b + 1) * LANES]
                if interval:
                    at = f * blocks + b
                    row = row - relaxation * returned[at : at + 1, :]
                table = jnp.broadcast_to(row, (PEERS, LANES))
                total_f = jnp.where(high == b, lookup(table, low), total_f)
            moved = pltpu.roll(
                jnp.concatenate([total_f, jnp.zeros((PEERS, LANES), F32)], axis=0), z + 1, 0
            )
            for r in range(3):
                outgoing[interval, f, r] = moved[GROUP * r : GROUP * (r + 1), :]

    def send_slots(interval):
        for r in range(3):
            for k in range(GROUP):
                f = lax.rem(z + k, GROUP)
                src = outgoing.at[interval, f, r]
                dst = arrived.at[interval, GROUP * (2 - r) + z]
                if r == 1 and k == 0:
                    pltpu.make_async_copy(src, dst, local.at[8 + interval]).start()
                else:
                    remote(
                        src, dst, flux_send.at[interval, GROUP * r + f],
                        flux_recv.at[interval, GROUP * (2 - r) + z],
                        base + GROUP * (r - 1) + f,
                    ).start()

    def receive_forcing(interval):
        for r in range(3):
            for k in range(GROUP):
                f = lax.rem(z + k, GROUP)
                src = outgoing.at[interval, f, r]
                dst = arrived.at[interval, GROUP * r + f]
                if r == 1 and k == 0:
                    pltpu.make_async_copy(src, dst, local.at[8 + interval]).wait()
                else:
                    copy = remote(
                        src, dst, flux_send.at[interval, GROUP * r + f],
                        flux_recv.at[interval, GROUP * r + f], base + GROUP * (r - 1) + f,
                    )
                    copy.wait_recv()
                    copy.wait_send()
    def cell_forcing(interval, i):
        for pair in range(cells // (2 * LANES)):
            cols = [slice((2 * pair + h) * LANES, (2 * pair + h + 1) * LANES) for h in range(2)]
            index = jnp.concatenate([slots[i, :, c] for c in cols], axis=0)
            weight = jnp.concatenate([weights[i, :, c] for c in cols], axis=0)
            low = index & (LANES - 1)
            high = lax.shift_right_logical(index, 7)
            value = jnp.zeros((PEERS, LANES), F32)
            for j in range(PEERS):
                row = arrived[interval, 7 + i - j, i : i + 1, :]
                table = jnp.broadcast_to(row, (PEERS, LANES))
                value = jnp.where(high == j, lookup(table, low), value)
            value = value * weight
            for h in range(2):
                added[i, :, cols[h]] = jnp.sum(value[4 * h : 4 * h + 4], axis=0, keepdims=True)

    def slot_sums(interval, i):
        place = lax.broadcasted_iota(jnp.int32, (PEERS, cells), 0)
        acc = jnp.zeros((2 * PEERS, LANES), F32)
        top = state[i, 0:1, :]
        for k in range(slots.shape[1]):
            hit = lax.shift_right_logical(slots[i, k : k + 1, :], 7) == place
            high, low = split(jnp.where(hit, weights[i, k : k + 1, :] * top, 0.0))
            acc = acc + across(jnp.concatenate([high, low], axis=0), slot_lanes[i, k])
        acc = acc[:PEERS] + acc[PEERS:]
        for j in range(PEERS):
            sums[interval, i - j + REACH + GROUP, i] = acc[j : j + 1, :]

    def back_copy(interval, r, k, start):
        f = lax.rem(z + k, GROUP)
        src = sums.at[interval, GROUP * r + f]
        if r == 1 and k == 0:
            dst = back.at[interval, GROUP + z]
            copy = pltpu.make_async_copy(src, dst, local.at[10 + interval])
            copy.start() if start else copy.wait()
            return
        send = back_send.at[interval, GROUP * r + f]
        p = base + GROUP * (r - 1) + f
        slot = GROUP * (2 - r) + z if start else GROUP * r + f
        copy = remote(src, back.at[interval, slot], send, back_recv.at[interval, slot], p)
        if start:
            copy.start()
        else:
            copy.wait_recv()
            copy.wait_send()

    def sums_out(interval):
        for r in range(3):
            for k in range(GROUP):
                back_copy(interval, r, k, True)

    def collect(interval):
        for r in range(3):
            for k in range(GROUP):
                back_copy(interval, r, k, False)
        place = lax.broadcasted_iota(jnp.int32, (blocks, LANES), 0)
        values = []
        for f in range(fields):
            rows = [back[interval, GROUP * r + f, i] for r in range(3) for i in range(GROUP)]
            rows.append(jnp.zeros((GROUP, LANES), F32))
            values.append(pltpu.roll(jnp.concatenate(rows, axis=0), 2 * PEERS - 1 - z, 0))
        columns = []
        for j in range(PEERS):
            hit = lax.shift_right_logical(sends[:, j * LANES : (j + 1) * LANES], 7) == place
            columns.append(
                jnp.concatenate(
                    [jnp.where(hit, values[f][j : j + 1, :], 0.0) for f in range(fields)], axis=0
                )
            )
        high, low = split(jnp.concatenate(columns, axis=1))
        both = across(jnp.concatenate([high, low], axis=0), point_lanes[...])
        returned[...] = both[: fields * blocks] + both[fields * blocks :]

    def set_parts(i, value):
        high, low = split(value)
        parts[i, 0:levels, 0:cells] = high
        parts[i, levels : 2 * levels, 0:cells] = low

    def rim_copy(t, side, c):
        a, b = PIECES[c]
        return remote(
            rim_out.at[t, side, a:b], rim_in.at[t, 1 - side, a:b], rim_send.at[t, side, c],
            rim_recv.at[t, 1 - side, c], me + (GROUP if side else -GROUP),
        )

    def outer_rims(t, side, c):
        i = side * (GROUP - 1)
        a, b = PIECES[c]
        both = jnp.concatenate(
            [parts[i, a:b, 0:cells], parts[i, levels + a : levels + b, 0:cells]], axis=0
        )
        edge = jnp.dot(
            both, rims[i, :, side * rim : (side + 1) * rim], preferred_element_type=F32
        )
        rim_out[t, side, a:b] = edge[0 : b - a] + edge[b - a :]
        rim_copy(t, side, c).start()

    def inner_rims(i):
        for side in range(2):
            j = i - 1 + 2 * side
            if 0 <= j < GROUP:
                edge = jnp.dot(
                    parts[i, :, 0:cells], rims[i, :, side * rim : (side + 1) * rim],
                    preferred_element_type=F32,
                )
                start = cells if side else cells + rim
                parts[j, :, start : start + rim] = edge.astype(BF16)

    def rim_arrives(t, side, c):
        a, b = PIECES[c]
        p = me + (GROUP if side else -GROUP)
        copy = remote(
            rim_out.at[t, 1 - side, a:b], rim_in.at[t, side, a:b], rim_send.at[t, 1 - side, c],
            rim_recv.at[t, side, c], p,
        )
        copy.wait_recv()
        high, low = split(rim_in[t, side, a:b])
        i, start = (GROUP - 1, cells + rim) if side else (0, cells)
        both = jnp.dot(
            jnp.concatenate([high, low], axis=0), wide_hi[i, start : start + rim, :],
            preferred_element_type=F32,
        )
        small = jnp.dot(high, wide_lo[i, start : start + rim, :], preferred_element_type=F32)
        return early[side, a:b] + (both[0 : b - a] + both[b - a :] + small)

    def rims_sent(t):
        for side in range(2):
            for c in range(len(PIECES)):
                rim_copy(t, side, c).wait_send()

    def product(i, first, last):
        both = jnp.dot(
            parts[i, :, first:last], wide_hi[i, first:last, :], preferred_element_type=F32
        )
        small = jnp.dot(
            parts[i, 0:levels, first:last], wide_lo[i, first:last, :], preferred_element_type=F32
        )
        return both[0:levels] + both[levels:] + small

    def mixed(i):
        here = state[i]
        row = lax.broadcasted_iota(jnp.int32, (levels, cells), 0)
        above = jnp.where(row == 0, here, pltpu.roll(here, 1, 0))
        below = jnp.where(row == levels - 1, here, pltpu.roll(here, levels - 1, 0))
        value = keep[i] * here + vertical_mix * (above + below)
        if i == 0:
            return value + product(i, 0, cells) + product(i, cells + rim, cells + 2 * rim)
        if i == GROUP - 1:
            return value + product(i, 0, cells + rim)
        return value + product(i, 0, cells + 2 * rim)

    def push(i):
        return added[i] * profile[...]

    pl.semaphore_wait(barrier, 3 * GROUP - 1)
    for d in range(1, GROUP):
        far = lax.rem(z + d, GROUP)
        for n, (src, dst) in enumerate(tables):
            remote(src, dst.at[z], table_send.at[n, far], table_recv.at[n, z], base + far).start()
    for d in range(1, GROUP):
        far = lax.rem(z + d, GROUP)
        remote(ocean.at[far], state.at[z], state_send.at[far], state_recv.at[z], base + far).start()
    sums[...] = jnp.zeros_like(sums)
    level = lax.broadcasted_iota(jnp.int32, (levels, cells), 0).astype(F32)
    profile[...] = forcing_scale * jnp.exp(-level / penetration)
    own[0].wait()
    own[1].wait()
    sends8[...] = jnp.concatenate(
        [sends[:, j * LANES : (j + 1) * LANES] for j in range(PEERS)], axis=0
    )
    gather(0)
    send_slots(0)
    for copy in own[3:]:
        copy.wait()
    step = 32

    def build_rims(i):
        def select(c, _):
            first = pl.multiple_of(c * step, step)
            place = lax.broadcasted_iota(jnp.int32, (step, rim), 0) + first
            for side in range(2):
                hit = halo[i, side : side + 1, :] == place
                rims[i, pl.ds(first, step), side * rim : (side + 1) * rim] = jnp.where(
                    hit, 1.0, 0.0
                ).astype(BF16)
            return 0

        lax.fori_loop(0, cells // step, select, 0)

    build_rims(z)

    def owner_copy(side, f, c):
        a, b = PIECES[c]
        return remote(
            owner_rims.at[f, a:b], rim_in.at[0, 1 - side, a:b], owner_send.at[f, c],
            rim_recv.at[0, 1 - side, c], base + (GROUP if side else -GROUP) + f,
        )

    def at_ends(act):
        for side in range(2):
            @pl.when(z == side * (GROUP - 1))
            def _():
                act(side)

    def first_rims(side):
        for f in range(fields):
            high, low = split(owner_state[f])
            edge = jnp.dot(
                jnp.concatenate([high, low], axis=0),
                rims[z, :, side * rim : (side + 1) * rim],
                preferred_element_type=F32,
            )
            owner_rims[f] = edge[0:levels] + edge[levels:]

    def first_rims_go(side):
        for c in range(len(PIECES)):
            for f in range(fields):
                owner_copy(side, f, c).start()

    def first_rims_sent(side):
        for c in range(len(PIECES)):
            for f in range(fields):
                owner_copy(side, f, c).wait_send()

    at_ends(first_rims)
    at_ends(first_rims_go)

    def build(i):
        rows = [coeff[i, n : n + 1, :] for n in range(near.shape[1])]
        ids = [near[i, n : n + 1, :] for n in range(near.shape[1])]
        summed = []
        for n in range(len(rows)):
            value = rows[n]
            for m in range(n):
                value = value + jnp.where(ids[m] == ids[n], rows[m], 0.0)
            summed.append(value)
        whole = rows[0]
        for n in range(1, len(rows)):
            whole = whole + rows[n]
        keep[i] = (1.0 - 2.0 * vertical_mix) - whole

        def fill(c, _):
            first = pl.multiple_of(c * step, step)
            for q in range(cells // LANES):
                cols = slice(q * LANES, (q + 1) * LANES)
                place = lax.broadcasted_iota(jnp.int32, (step, LANES), 0) + first
                value = jnp.zeros((step, LANES), F32)
                for n in range(len(rows)):
                    value = jnp.where(ids[n][:, cols] == place, summed[n][:, cols], value)
                high, low = split(value)
                wide_hi[i, pl.ds(first, step), cols] = high
                wide_lo[i, pl.ds(first, step), cols] = low
            return 0

        lax.fori_loop(0, (cells + 2 * rim) // step, fill, 0)

        @pl.when(i != z)
        def _():
            build_rims(i)

        place = lax.broadcasted_iota(jnp.int32, (LANES, cells), 0)
        for k in range(slots.shape[1]):
            hit = (slots[i, k : k + 1, :] & (LANES - 1)) == place
            slot_lanes[i, k] = jnp.where(hit, 1.0, 0.0).astype(BF16)

    def build_all(d, _):
        i = lax.rem(z + d, GROUP)

        @pl.when(d > 0)
        def _():
            for n, (src, dst) in enumerate(tables):
                copy = remote(src, dst.at[i], table_send.at[n, i], table_recv.at[n, i], base + i)
                copy.wait_recv()
                copy.wait_send()

        build(i)
        return 0

    lax.fori_loop(0, GROUP, build_all, 0)

    place = lax.broadcasted_iota(jnp.int32, (LANES, cells), 0)
    for h in range(sends.shape[1] // cells):
        hit = (sends[:, h * cells : (h + 1) * cells] & (LANES - 1)) == place
        point_lanes[:, h * cells : (h + 1) * cells] = jnp.where(hit, 1.0, 0.0).astype(BF16)

    own[2].wait()
    set_parts(z, state[z])
    for d in range(1, GROUP):
        far = lax.rem(z + d, GROUP)
        copy = remote(
            ocean.at[far], state.at[far], state_send.at[far], state_recv.at[far], base + far
        )
        copy.wait_recv()
        copy.wait_send()
        set_parts(far, state[far])
    pieces = range(len(PIECES))

    for i in (0, 3, 1, 2):
        inner_rims(i)

    def settle(i, value):
        state[i] = value
        set_parts(i, value)

    def settle_piece(i, c, value):
        a, b = PIECES[c]
        high, low = split(value)
        state[i, a:b] = value
        parts[i, a:b, 0:cells] = high
        parts[i, levels + a : levels + b, 0:cells] = low

    def first(interval):
        t = STEPS * interval
        early[0] = mixed(0)
        early[1] = mixed(3)
        for i in (1, 2):
            state[i] = mixed(i)
        if interval:
            collect(0)
            gather(1)
            send_slots(1)
        for c in pieces:
            a, b = PIECES[c]
            state[0, a:b] = rim_arrives(t, 0, c)
            state[3, a:b] = rim_arrives(t, 1, c)
        receive_forcing(interval)
        for i in (0, 3):
            cell_forcing(interval, i)
            settle(i, state[i] + push(i))
        for c in pieces:
            outer_rims(t + 1, 0, c)
            outer_rims(t + 1, 1, c)
        for i in (1, 2):
            cell_forcing(interval, i)
            settle(i, state[i] + push(i))
        for i in (0, 3, 1, 2):
            inner_rims(i)
        if interval:
            rims_sent(t)
        else:
            at_ends(first_rims_sent)

    def plain(t, sums_too=False):
        for i in (1, 2):
            settle(i, mixed(i) + push(i))
        early[0] = mixed(0) + push(0)
        early[1] = mixed(3) + push(3)
        if sums_too:
            slot_sums(0, 1)
            slot_sums(0, 2)
        for c in pieces:
            for side in range(2):
                settle_piece(side * (GROUP - 1), c, rim_arrives(t, side, c))
                outer_rims(t + 1, side, c)
            if sums_too and c == 0:
                slot_sums(0, 0)
                slot_sums(0, 3)
                sums_out(0)
        for i in (0, 3, 1, 2):
            inner_rims(i)
        rims_sent(t)

    def ship(i):
        @pl.when(z == i)
        def _():
            pltpu.make_async_copy(state.at[i], out_state.at[i], local.at[14]).start()

        @pl.when(z != i)
        def _():
            remote(
                state.at[i], out_state.at[z], out_send.at[i], out_recv.at[z], base + i
            ).start()

    first(0)
    for t in range(1, STEPS):
        plain(t, t == STEPS - 1)
    first(1)
    plain(STEPS + 1)
    last = 2 * STEPS - 1
    for i in (1, 2):
        state[i] = mixed(i) + push(i)
        slot_sums(1, i)
        state[i] = 0.5 * state[i]
        ship(i)
    early[0] = mixed(0) + push(0)
    early[1] = mixed(3) + push(3)
    for c in pieces:
        a, b = PIECES[c]
        state[0, a:b] = rim_arrives(last, 0, c)
        state[3, a:b] = rim_arrives(last, 1, c)
        if c == 0:
            slot_sums(1, 0)
            slot_sums(1, 3)
            sums_out(1)
    for i in (0, 3):
        state[i] = 0.5 * state[i]
        ship(i)
    rims_sent(last)
    collect(1)
    for b in range(blocks):
        out_atm[:, b * LANES : (b + 1) * LANES] = jnp.concatenate(
            [returned[f * blocks + b : f * blocks + b + 1, :] for f in range(fields)], axis=0
        )
    pltpu.make_async_copy(state.at[z], out_state.at[z], local.at[14]).wait()
    for d in range(1, GROUP):
        far = lax.rem(z + d, GROUP)
        copy = remote(
            state.at[far], out_state.at[far], out_send.at[far], out_recv.at[far], base + far
        )
        copy.wait_recv()
        copy.wait_send()


def shards(
    ocean_state, atm_flux, edge_coeff, neighbours, halo_send, send_idx, recv_slot, regrid_weight
):
    fields, levels, cells = ocean_state.shape
    points = atm_flux.shape[2]
    rim = halo_send.shape[1]
    slot_count = send_idx.shape[1]
    near = neighbours.shape[0]
    sources = recv_slot.shape[0]
    wide = cells + 2 * rim
    steps = 2 * STEPS
    dma = pltpu.SemaphoreType.DMA
    final, atm = pl.pallas_call(
        kernel,
        out_shape=(
            jax.ShapeDtypeStruct((fields, levels, cells), F32),
            jax.ShapeDtypeStruct((fields, points), F32),
        ),
        in_specs=[pl.BlockSpec(memory_space=pltpu.HBM)] * 8,
        out_specs=(
            pl.BlockSpec(memory_space=pl.ANY),
            pl.BlockSpec(memory_space=pltpu.VMEM),
        ),
        scratch_shapes=[
            pltpu.VMEM((GROUP, levels, cells), F32),
            pltpu.VMEM((GROUP, 2 * levels, wide), BF16),
            pltpu.VMEM((GROUP, wide, cells), BF16),
            pltpu.VMEM((GROUP, wide, cells), BF16),
            pltpu.VMEM((GROUP, cells, 2 * rim), BF16),
            pltpu.VMEM((GROUP, near, cells), F32),
            pltpu.VMEM((GROUP, near, cells), jnp.int32),
            pltpu.VMEM((GROUP, 2, rim), jnp.int32),
            pltpu.VMEM((GROUP, sources, cells), jnp.int32),
            pltpu.VMEM((GROUP, sources, cells), F32),
            pltpu.VMEM((1, slot_count), jnp.int32),
            pltpu.VMEM((2, fields, points), F32),
            pltpu.VMEM((PEERS, LANES), jnp.int32),
            pltpu.VMEM((GROUP, 1, cells), F32),
            pltpu.VMEM((levels, cells), F32),
            pltpu.VMEM((GROUP, 1, cells), F32),
            pltpu.VMEM((GROUP, sources, LANES, cells), BF16),
            pltpu.VMEM((LANES, slot_count), BF16),
            pltpu.VMEM((2, fields, 3, GROUP, LANES), F32),
            pltpu.VMEM((2, 3 * GROUP, GROUP, LANES), F32),
            pltpu.VMEM((2, 3 * GROUP, GROUP, 1, LANES), F32),
            pltpu.VMEM((2, 3 * GROUP, GROUP, 1, LANES), F32),
            pltpu.VMEM((fields * points // LANES, LANES), F32),
            pltpu.VMEM((steps, 2, levels, rim), F32),
            pltpu.VMEM((steps, 2, levels, rim), F32),
            pltpu.VMEM((2, levels, cells), F32),
            pltpu.VMEM((fields, levels, cells), F32),
            pltpu.VMEM((fields, levels, rim), F32),
            dma((GROUP,)),
            dma((GROUP,)),
            dma((5, GROUP)),
            dma((5, GROUP)),
            dma((2, 3 * GROUP)),
            dma((2, 3 * GROUP)),
            dma((2, 3 * GROUP)),
            dma((2, 3 * GROUP)),
            dma((steps, 2, len(PIECES))),
            dma((steps, 2, len(PIECES))),
            dma((fields, len(PIECES))),
            dma((GROUP,)),
            dma((GROUP,)),
            dma((16,)),
        ],
        compiler_params=pltpu.CompilerParams(
            collective_id=0, has_side_effects=True, vmem_limit_bytes=67_043_328
        ),
        name="coupled",
    )(
        ocean_state, atm_flux, edge_coeff, neighbours, halo_send, send_idx, recv_slot,
        regrid_weight,
    )
    return 2.0 * final, atm


def solution(mesh):
    placed = (
        P(None, None, AXES),
        P(None, None, AXES),
        P(None, AXES),
        P(None, AXES),
        P(None, AXES),
        P(AXES, None),
        P(None, AXES),
        P(None, AXES),
    )
    return jax.shard_map(
        shards,
        mesh=mesh,
        in_specs=placed,
        out_specs=(P(None, None, AXES), P(None, AXES)),
        check_vma=False,
    )
```

```python
import jax
import jax.numpy as jnp
from jax import lax
from jax.experimental import pallas as pl
from jax.experimental.pallas import tpu as pltpu
from jax.sharding import PartitionSpec as P

AXES = ("comp", "dom")
MESH = pl.DeviceIdType.MESH
F32 = jnp.float32
BF16 = jnp.bfloat16

PEERS = 8
REACH = 3
STEPS = 3
GROUP = 4
LANES = 128
PIECES = ((0, 80),)

vertical_mix = 0.2
forcing_scale = 0.1
relaxation = 0.25
penetration = 8.0


def split(value):
    high = value.astype(BF16)
    return high, (value - high.astype(F32)).astype(BF16)


def across(left, right):
    return lax.dot_general(left, right, (((1,), (1,)), ((), ())), preferred_element_type=F32)


def lookup(table, index):
    return jnp.take_along_axis(table, index, axis=1, mode="promise_in_bounds")


def kernel(
    ocean, flux, coeff_in, near_in, halo_in, send_in, slot_in, weight_in,
    out_state, out_atm,
    state, parts, wide_hi, wide_lo, rims, coeff, near, halo, slots, weights,
    sends, air, sends8, keep, profile, added,
    slot_lanes, point_lanes, outgoing, arrived, sums, back, returned,
    rim_out, rim_in, early, owner_state, owner_rims,
    state_send, state_recv, table_send, table_recv, flux_send, flux_recv,
    back_send, back_recv, rim_send, rim_recv, owner_send, out_send, out_recv, local,
):
    levels, cells = state.shape[1:]
    rim = halo.shape[2]
    points = air.shape[2]
    fields = GROUP
    blocks = points // LANES
    doms = lax.axis_size("dom")
    total = lax.axis_size("comp") * doms
    me = lax.axis_index("comp") * doms + lax.axis_index("dom")
    z = lax.rem(me, GROUP)
    base = me - z

    def device(p):
        p = lax.rem(p + total, total)
        return (lax.div(p, doms), lax.rem(p, doms))

    def remote(src, dst, send, recv, p):
        return pltpu.make_async_remote_copy(
            src_ref=src, dst_ref=dst, send_sem=send, recv_sem=recv,
            device_id=device(p), device_id_type=MESH,
        )

    barrier = pltpu.get_barrier_semaphore()
    for r in range(3):
        for k in range(GROUP):
            if r == 1 and k == 0:
                continue
            far = base + GROUP * (r - 1) + lax.rem(z + k, GROUP)
            pl.semaphore_signal(barrier, inc=1, device_id=device(far), device_id_type=MESH)

    tables = [(coeff_in, coeff), (near_in, near), (halo_in, halo), (slot_in, slots), (weight_in, weights)]
    own = [
        pltpu.make_async_copy(send_in, sends, local.at[0]),
        pltpu.make_async_copy(flux, air, local.at[1]),
        pltpu.make_async_copy(ocean.at[z], state.at[z], local.at[2]),
    ] + [
        pltpu.make_async_copy(src, dst.at[z], local.at[3 + n])
        for n, (src, dst) in enumerate(tables)
    ] + [pltpu.make_async_copy(ocean, owner_state, local.at[15])]
    for copy in own:
        copy.start()

    def gather(interval):
        low = sends8[...] & (LANES - 1)
        high = lax.shift_right_logical(sends8[...], 7)
        for f in range(fields):
            total_f = jnp.zeros((PEERS, LANES), F32)
            for b in range(blocks):
                row = air[interval, f : f + 1, b * LANES : (b + 1) * LANES]
                if interval:
                    at = f * blocks + b
                    row = row - relaxation * returned[at : at + 1, :]
                table = jnp.broadcast_to(row, (PEERS, LANES))
                total_f = jnp.where(high == b, lookup(table, low), total_f)
            moved = pltpu.roll(
                jnp.concatenate([total_f, jnp.zeros((PEERS, LANES), F32)], axis=0), z + 1, 0
            )
            for r in range(3):
                outgoing[interval, f, r] = moved[GROUP * r : GROUP * (r + 1), :]

    def send_slots(interval):
        for r in range(3):
            for k in range(GROUP):
                f = lax.rem(z + k, GROUP)
                src = outgoing.at[interval, f, r]
                dst = arrived.at[interval, GROUP * (2 - r) + z]
                if r == 1 and k == 0:
                    pltpu.make_async_copy(src, dst, local.at[8 + interval]).start()
                else:
                    remote(
                        src, dst, flux_send.at[interval, GROUP * r + f],
                        flux_recv.at[interval, GROUP * (2 - r) + z],
                        base + GROUP * (r - 1) + f,
                    ).start()

    def receive_forcing(interval):
        for r in range(3):
            for k in range(GROUP):
                f = lax.rem(z + k, GROUP)
                src = outgoing.at[interval, f, r]
                dst = arrived.at[interval, GROUP * r + f]
                if r == 1 and k == 0:
                    pltpu.make_async_copy(src, dst, local.at[8 + interval]).wait()
                else:
                    copy = remote(
                        src, dst, flux_send.at[interval, GROUP * r + f],
                        flux_recv.at[interval, GROUP * r + f], base + GROUP * (r - 1) + f,
                    )
                    copy.wait_recv()
                    copy.wait_send()
    def cell_forcing(interval, i):
        for pair in range(cells // (2 * LANES)):
            cols = [slice((2 * pair + h) * LANES, (2 * pair + h + 1) * LANES) for h in range(2)]
            index = jnp.concatenate([slots[i, :, c] for c in cols], axis=0)
            weight = jnp.concatenate([weights[i, :, c] for c in cols], axis=0)
            low = index & (LANES - 1)
            high = lax.shift_right_logical(index, 7)
            value = jnp.zeros((PEERS, LANES), F32)
            for j in range(PEERS):
                row = arrived[interval, 7 + i - j, i : i + 1, :]
                table = jnp.broadcast_to(row, (PEERS, LANES))
                value = jnp.where(high == j, lookup(table, low), value)
            value = value * weight
            for h in range(2):
                added[i, :, cols[h]] = jnp.sum(value[4 * h : 4 * h + 4], axis=0, keepdims=True)

    def slot_sums(interval, i):
        place = lax.broadcasted_iota(jnp.int32, (PEERS, cells), 0)
        acc = jnp.zeros((2 * PEERS, LANES), F32)
        top = state[i, 0:1, :]
        for k in range(slots.shape[1]):
            hit = lax.shift_right_logical(slots[i, k : k + 1, :], 7) == place
            high, low = split(jnp.where(hit, weights[i, k : k + 1, :] * top, 0.0))
            acc = acc + across(jnp.concatenate([high, low], axis=0), slot_lanes[i, k])
        acc = acc[:PEERS] + acc[PEERS:]
        for j in range(PEERS):
            sums[interval, i - j + REACH + GROUP, i] = acc[j : j + 1, :]

    def back_copy(interval, r, k, start):
        f = lax.rem(z + k, GROUP)
        src = sums.at[interval, GROUP * r + f]
        if r == 1 and k == 0:
            dst = back.at[interval, GROUP + z]
            copy = pltpu.make_async_copy(src, dst, local.at[10 + interval])
            copy.start() if start else copy.wait()
            return
        send = back_send.at[interval, GROUP * r + f]
        p = base + GROUP * (r - 1) + f
        slot = GROUP * (2 - r) + z if start else GROUP * r + f
        copy = remote(src, back.at[interval, slot], send, back_recv.at[interval, slot], p)
        if start:
            copy.start()
        else:
            copy.wait_recv()
            copy.wait_send()

    def sums_out(interval):
        for r in range(3):
            for k in range(GROUP):
                back_copy(interval, r, k, True)

    def collect(interval):
        for r in range(3):
            for k in range(GROUP):
                back_copy(interval, r, k, False)
        place = lax.broadcasted_iota(jnp.int32, (blocks, LANES), 0)
        values = []
        for f in range(fields):
            rows = [back[interval, GROUP * r + f, i] for r in range(3) for i in range(GROUP)]
            rows.append(jnp.zeros((GROUP, LANES), F32))
            values.append(pltpu.roll(jnp.concatenate(rows, axis=0), 2 * PEERS - 1 - z, 0))
        columns = []
        for j in range(PEERS):
            hit = lax.shift_right_logical(sends[:, j * LANES : (j + 1) * LANES], 7) == place
            columns.append(
                jnp.concatenate(
                    [jnp.where(hit, values[f][j : j + 1, :], 0.0) for f in range(fields)], axis=0
                )
            )
        high, low = split(jnp.concatenate(columns, axis=1))
        both = across(jnp.concatenate([high, low], axis=0), point_lanes[...])
        returned[...] = both[: fields * blocks] + both[fields * blocks :]

    def set_parts(i, value):
        high, low = split(value)
        parts[i, 0:levels, 0:cells] = high
        parts[i, levels : 2 * levels, 0:cells] = low

    def rim_copy(t, side, c):
        a, b = PIECES[c]
        return remote(
            rim_out.at[t, side, a:b], rim_in.at[t, 1 - side, a:b], rim_send.at[t, side, c],
            rim_recv.at[t, 1 - side, c], me + (GROUP if side else -GROUP),
        )

    def outer_rims(t, side, c):
        i = side * (GROUP - 1)
        a, b = PIECES[c]
        both = jnp.concatenate(
            [parts[i, a:b, 0:cells], parts[i, levels + a : levels + b, 0:cells]], axis=0
        )
        edge = jnp.dot(
            both, rims[i, :, side * rim : (side + 1) * rim], preferred_element_type=F32
        )
        rim_out[t, side, a:b] = edge[0 : b - a] + edge[b - a :]
        rim_copy(t, side, c).start()

    def inner_rims(i):
        for side in range(2):
            j = i - 1 + 2 * side
            if 0 <= j < GROUP:
                edge = jnp.dot(
                    parts[i, :, 0:cells], rims[i, :, side * rim : (side + 1) * rim],
                    preferred_element_type=F32,
                )
                start = cells if side else cells + rim
                parts[j, :, start : start + rim] = edge.astype(BF16)

    def rim_arrives(t, side, c):
        a, b = PIECES[c]
        p = me + (GROUP if side else -GROUP)
        copy = remote(
            rim_out.at[t, 1 - side, a:b], rim_in.at[t, side, a:b], rim_send.at[t, 1 - side, c],
            rim_recv.at[t, side, c], p,
        )
        copy.wait_recv()
        high, low = split(rim_in[t, side, a:b])
        i, start = (GROUP - 1, cells + rim) if side else (0, cells)
        both = jnp.dot(
            jnp.concatenate([high, low], axis=0), wide_hi[i, start : start + rim, :],
            preferred_element_type=F32,
        )
        small = jnp.dot(high, wide_lo[i, start : start + rim, :], preferred_element_type=F32)
        return early[side, a:b] + (both[0 : b - a] + both[b - a :] + small)

    def rims_sent(t):
        for side in range(2):
            for c in range(len(PIECES)):
                rim_copy(t, side, c).wait_send()

    def product(i, first, last):
        both = jnp.dot(
            parts[i, :, first:last], wide_hi[i, first:last, :], preferred_element_type=F32
        )
        small = jnp.dot(
            parts[i, 0:levels, first:last], wide_lo[i, first:last, :], preferred_element_type=F32
        )
        return both[0:levels] + both[levels:] + small

    def mixed(i):
        here = state[i]
        row = lax.broadcasted_iota(jnp.int32, (levels, cells), 0)
        above = jnp.where(row == 0, here, pltpu.roll(here, 1, 0))
        below = jnp.where(row == levels - 1, here, pltpu.roll(here, levels - 1, 0))
        value = keep[i] * here + vertical_mix * (above + below)
        if i == 0:
            return value + product(i, 0, cells) + product(i, cells + rim, cells + 2 * rim)
        if i == GROUP - 1:
            return value + product(i, 0, cells + rim)
        return value + product(i, 0, cells + 2 * rim)

    def push(i):
        return added[i] * profile[...]

    sums[...] = jnp.zeros_like(sums)
    level = lax.broadcasted_iota(jnp.int32, (levels, cells), 0).astype(F32)
    profile[...] = forcing_scale * jnp.exp(-level / penetration)
    own[0].wait()
    own[1].wait()
    sends8[...] = jnp.concatenate(
        [sends[:, j * LANES : (j + 1) * LANES] for j in range(PEERS)], axis=0
    )
    gather(0)
    for copy in own[3:]:
        copy.wait()
    step = 32

    def build_rims(i):
        def select(c, _):
            first = pl.multiple_of(c * step, step)
            place = lax.broadcasted_iota(jnp.int32, (step, rim), 0) + first
            for side in range(2):
                hit = halo[i, side : side + 1, :] == place
                rims[i, pl.ds(first, step), side * rim : (side + 1) * rim] = jnp.where(
                    hit, 1.0, 0.0
                ).astype(BF16)
            return 0

        lax.fori_loop(0, cells // step, select, 0)

    build_rims(z)

    def owner_copy(side, f, c):
        a, b = PIECES[c]
        return remote(
            owner_rims.at[f, a:b], rim_in.at[0, 1 - side, a:b], owner_send.at[f, c],
            rim_recv.at[0, 1 - side, c], base + (GROUP if side else -GROUP) + f,
        )

    def at_ends(act):
        for side in range(2):
            @pl.when(z == side * (GROUP - 1))
            def _():
                act(side)

    def first_rims(side):
        for f in range(fields):
            high, low = split(owner_state[f])
            edge = jnp.dot(
                jnp.concatenate([high, low], axis=0),
                rims[z, :, side * rim : (side + 1) * rim],
                preferred_element_type=F32,
            )
            owner_rims[f] = edge[0:levels] + edge[levels:]

    def first_rims_go(side):
        for c in range(len(PIECES)):
            for f in range(fields):
                owner_copy(side, f, c).start()

    def first_rims_sent(side):
        for c in range(len(PIECES)):
            for f in range(fields):
                owner_copy(side, f, c).wait_send()

    at_ends(first_rims)
    pl.semaphore_wait(barrier, 3 * GROUP - 1)
    for d in range(1, GROUP):
        far = lax.rem(z + d, GROUP)
        for n, (src, dst) in enumerate(tables):
            remote(src, dst.at[z], table_send.at[n, far], table_recv.at[n, z], base + far).start()
    send_slots(0)
    for d in range(1, GROUP):
        far = lax.rem(z + d, GROUP)
        remote(ocean.at[far], state.at[z], state_send.at[far], state_recv.at[z], base + far).start()
    at_ends(first_rims_go)

    def build(i):
        rows = [coeff[i, n : n + 1, :] for n in range(near.shape[1])]
        ids = [near[i, n : n + 1, :] for n in range(near.shape[1])]
        summed = []
        for n in range(len(rows)):
            value = rows[n]
            for m in range(n):
                value = value + jnp.where(ids[m] == ids[n], rows[m], 0.0)
            summed.append(value)
        whole = rows[0]
        for n in range(1, len(rows)):
            whole = whole + rows[n]
        keep[i] = (1.0 - 2.0 * vertical_mix) - whole

        def fill(c, _):
            first = pl.multiple_of(c * step, step)
            for q in range(cells // LANES):
                cols = slice(q * LANES, (q + 1) * LANES)
                place = lax.broadcasted_iota(jnp.int32, (step, LANES), 0) + first
                value = jnp.zeros((step, LANES), F32)
                for n in range(len(rows)):
                    value = jnp.where(ids[n][:, cols] == place, summed[n][:, cols], value)
                high, low = split(value)
                wide_hi[i, pl.ds(first, step), cols] = high
                wide_lo[i, pl.ds(first, step), cols] = low
            return 0

        lax.fori_loop(0, (cells + 2 * rim) // step, fill, 0)

        @pl.when(i != z)
        def _():
            build_rims(i)

        place = lax.broadcasted_iota(jnp.int32, (LANES, cells), 0)
        for k in range(slots.shape[1]):
            hit = (slots[i, k : k + 1, :] & (LANES - 1)) == place
            slot_lanes[i, k] = jnp.where(hit, 1.0, 0.0).astype(BF16)

    def build_all(d, _):
        i = lax.rem(z + d, GROUP)

        @pl.when(d > 0)
        def _():
            for n, (src, dst) in enumerate(tables):
                copy = remote(src, dst.at[i], table_send.at[n, i], table_recv.at[n, i], base + i)
                copy.wait_recv()
                copy.wait_send()

        build(i)
        return 0

    lax.fori_loop(0, GROUP, build_all, 0)

    place = lax.broadcasted_iota(jnp.int32, (LANES, cells), 0)
    for h in range(sends.shape[1] // cells):
        hit = (sends[:, h * cells : (h + 1) * cells] & (LANES - 1)) == place
        point_lanes[:, h * cells : (h + 1) * cells] = jnp.where(hit, 1.0, 0.0).astype(BF16)

    own[2].wait()
    set_parts(z, state[z])
    for d in range(1, GROUP):
        far = lax.rem(z + d, GROUP)
        copy = remote(
            ocean.at[far], state.at[far], state_send.at[far], state_recv.at[far], base + far
        )
        copy.wait_recv()
        copy.wait_send()
        set_parts(far, state[far])
    pieces = range(len(PIECES))

    for i in (0, 3, 1, 2):
        inner_rims(i)

    def settle(i, value):
        state[i] = value
        set_parts(i, value)

    def settle_piece(i, c, value):
        a, b = PIECES[c]
        high, low = split(value)
        state[i, a:b] = value
        parts[i, a:b, 0:cells] = high
        parts[i, levels + a : levels + b, 0:cells] = low

    def first(interval):
        t = STEPS * interval
        early[0] = mixed(0)
        early[1] = mixed(3)
        for i in (1, 2):
            state[i] = mixed(i)
        if interval:
            collect(0)
            gather(1)
            send_slots(1)
        for c in pieces:
            a, b = PIECES[c]
            state[0, a:b] = rim_arrives(t, 0, c)
            state[3, a:b] = rim_arrives(t, 1, c)
        receive_forcing(interval)
        for i in (0, 3):
            cell_forcing(interval, i)
            settle(i, state[i] + push(i))
        for c in pieces:
            outer_rims(t + 1, 0, c)
            outer_rims(t + 1, 1, c)
        for i in (1, 2):
            cell_forcing(interval, i)
            settle(i, state[i] + push(i))
        for i in (0, 3, 1, 2):
            inner_rims(i)
        if interval:
            rims_sent(t)
        else:
            at_ends(first_rims_sent)

    def plain(t, sums_too=False):
        for i in (1, 2):
            settle(i, mixed(i) + push(i))
        early[0] = mixed(0) + push(0)
        early[1] = mixed(3) + push(3)
        if sums_too:
            slot_sums(0, 1)
            slot_sums(0, 2)
        for c in pieces:
            for side in range(2):
                settle_piece(side * (GROUP - 1), c, rim_arrives(t, side, c))
                outer_rims(t + 1, side, c)
            if sums_too and c == 0:
                slot_sums(0, 0)
                slot_sums(0, 3)
                sums_out(0)
        for i in (0, 3, 1, 2):
            inner_rims(i)
        rims_sent(t)

    def ship(i):
        @pl.when(z == i)
        def _():
            pltpu.make_async_copy(state.at[i], out_state.at[i], local.at[14]).start()

        @pl.when(z != i)
        def _():
            remote(
                state.at[i], out_state.at[z], out_send.at[i], out_recv.at[z], base + i
            ).start()

    first(0)
    for t in range(1, STEPS):
        plain(t, t == STEPS - 1)
    first(1)
    plain(STEPS + 1)
    last = 2 * STEPS - 1
    for i in (1, 2):
        state[i] = mixed(i) + push(i)
        slot_sums(1, i)
        state[i] = 0.5 * state[i]
        ship(i)
    early[0] = mixed(0) + push(0)
    early[1] = mixed(3) + push(3)
    for c in pieces:
        a, b = PIECES[c]
        state[0, a:b] = rim_arrives(last, 0, c)
        state[3, a:b] = rim_arrives(last, 1, c)
        if c == 0:
            slot_sums(1, 0)
            slot_sums(1, 3)
            sums_out(1)
    for i in (0, 3):
        state[i] = 0.5 * state[i]
        ship(i)
    rims_sent(last)
    collect(1)
    for b in range(blocks):
        out_atm[:, b * LANES : (b + 1) * LANES] = jnp.concatenate(
            [returned[f * blocks + b : f * blocks + b + 1, :] for f in range(fields)], axis=0
        )
    pltpu.make_async_copy(state.at[z], out_state.at[z], local.at[14]).wait()
    for d in range(1, GROUP):
        far = lax.rem(z + d, GROUP)
        copy = remote(
            state.at[far], out_state.at[far], out_send.at[far], out_recv.at[far], base + far
        )
        copy.wait_recv()
        copy.wait_send()


def shards(
    ocean_state, atm_flux, edge_coeff, neighbours, halo_send, send_idx, recv_slot, regrid_weight
):
    fields, levels, cells = ocean_state.shape
    points = atm_flux.shape[2]
    rim = halo_send.shape[1]
    slot_count = send_idx.shape[1]
    near = neighbours.shape[0]
    sources = recv_slot.shape[0]
    wide = cells + 2 * rim
    steps = 2 * STEPS
    dma = pltpu.SemaphoreType.DMA
    final, atm = pl.pallas_call(
        kernel,
        out_shape=(
            jax.ShapeDtypeStruct((fields, levels, cells), F32),
            jax.ShapeDtypeStruct((fields, points), F32),
        ),
        in_specs=[pl.BlockSpec(memory_space=pltpu.HBM)] * 8,
        out_specs=(
            pl.BlockSpec(memory_space=pl.ANY),
            pl.BlockSpec(memory_space=pltpu.VMEM),
        ),
        scratch_shapes=[
            pltpu.VMEM((GROUP, levels, cells), F32),
            pltpu.VMEM((GROUP, 2 * levels, wide), BF16),
            pltpu.VMEM((GROUP, wide, cells), BF16),
            pltpu.VMEM((GROUP, wide, cells), BF16),
            pltpu.VMEM((GROUP, cells, 2 * rim), BF16),
            pltpu.VMEM((GROUP, near, cells), F32),
            pltpu.VMEM((GROUP, near, cells), jnp.int32),
            pltpu.VMEM((GROUP, 2, rim), jnp.int32),
            pltpu.VMEM((GROUP, sources, cells), jnp.int32),
            pltpu.VMEM((GROUP, sources, cells), F32),
            pltpu.VMEM((1, slot_count), jnp.int32),
            pltpu.VMEM((2, fields, points), F32),
            pltpu.VMEM((PEERS, LANES), jnp.int32),
            pltpu.VMEM((GROUP, 1, cells), F32),
            pltpu.VMEM((levels, cells), F32),
            pltpu.VMEM((GROUP, 1, cells), F32),
            pltpu.VMEM((GROUP, sources, LANES, cells), BF16),
            pltpu.VMEM((LANES, slot_count), BF16),
            pltpu.VMEM((2, fields, 3, GROUP, LANES), F32),
            pltpu.VMEM((2, 3 * GROUP, GROUP, LANES), F32),
            pltpu.VMEM((2, 3 * GROUP, GROUP, 1, LANES), F32),
            pltpu.VMEM((2, 3 * GROUP, GROUP, 1, LANES), F32),
            pltpu.VMEM((fields * points // LANES, LANES), F32),
            pltpu.VMEM((steps, 2, levels, rim), F32),
            pltpu.VMEM((steps, 2, levels, rim), F32),
            pltpu.VMEM((2, levels, cells), F32),
            pltpu.VMEM((fields, levels, cells), F32),
            pltpu.VMEM((fields, levels, rim), F32),
            dma((GROUP,)),
            dma((GROUP,)),
            dma((5, GROUP)),
            dma((5, GROUP)),
            dma((2, 3 * GROUP)),
            dma((2, 3 * GROUP)),
            dma((2, 3 * GROUP)),
            dma((2, 3 * GROUP)),
            dma((steps, 2, len(PIECES))),
            dma((steps, 2, len(PIECES))),
            dma((fields, len(PIECES))),
            dma((GROUP,)),
            dma((GROUP,)),
            dma((16,)),
        ],
        compiler_params=pltpu.CompilerParams(
            collective_id=0, has_side_effects=True, vmem_limit_bytes=67_043_328
        ),
        name="coupled",
    )(
        ocean_state, atm_flux, edge_coeff, neighbours, halo_send, send_idx, recv_slot,
        regrid_weight,
    )
    return 2.0 * final, atm


def solution(mesh):
    placed = (
        P(None, None, AXES),
        P(None, None, AXES),
        P(None, AXES),
        P(None, AXES),
        P(None, AXES),
        P(AXES, None),
        P(None, AXES),
        P(None, AXES),
    )
    return jax.shard_map(
        shards,
        mesh=mesh,
        in_specs=placed,
        out_specs=(P(None, None, AXES), P(None, AXES)),
        check_vma=False,
    )
```
